256 devices in a mesh: grp: 32 (over x, y, core), blk: 8 (over z).
Axes of the slice: x: 4, y: 4, z: 8, core: 2. Of those that a mesh axis runs over, the one named last changes fastest.
Arguments:
- tiles_near: bfloat16 [16384, 256, 256], P(('grp', 'blk')), may hold values from -0.078125 to 0.078125
- near_cols: int32 [256, 64], P(('grp', 'blk')), may hold values from 0 to 3
- tiles_far: bfloat16 [6144, 256, 256], P(('grp', 'blk')), may hold values from -0.078125 to 0.078125
- far_groups: int32 [256, 24], P(('grp', 'blk')), may hold values from 0 to 31, as said below
- need_blocks: int32 [256, 32], P(('grp', 'blk')), may hold values from -1 to 3, as said below
- start_vectors: bfloat16 [262144, 128], P(('grp', 'blk')), may hold values from -6 to 6
Outputs:
- vectors: float32 [262144, 128], P(('grp', 'blk'))
The draws below stay inside these ranges and needn't reach their ends.
Inputs may be any that keep to these rules, and one draw needn't show every extreme that they name: need_blocks[d, h] is -1 for d's own group and for groups d reads nothing from, else a row block index below 4 of the device of group h at d's position along blk; every device reads from at least one other group. far_groups[d, t] is a group h with need_blocks[d, h] >= 0.
All inputs are finite; a program needn't handle non-finite values.
Results may differ from the reference program's by a relative error of at most 0.0029.
Values may be sent and summed in bfloat16 or wider, within the bound.
A program may use at most 128 MiB of HBM per device.

```python
import jax
import jax.numpy as jnp
from jax import lax

K = 128
TILE = 256
RB_DEV = 4
NPS = 2
FAR_RB = 6
ITERS = 2
NB = 1024
ROWS = 262144
TN = 64
TF = 24
N_GRP = 32
N_BLK = 8
DEVICES = 256


def linked_draw(key):
    folded = jax.random.fold_in(key, 11)
    key_named, key_block, key_picked = jax.random.split(folded, 3)
    device = jnp.arange(DEVICES, dtype=jnp.int32)
    group_id = device // N_BLK
    groups = jnp.arange(N_GRP, dtype=jnp.int32)
    named = jax.random.randint(key_named, (DEVICES, N_GRP), 0, 10) < 6
    named = named & (groups[None, :] != group_id[:, None])
    named = named | (groups[None, :] == ((group_id + 1) % N_GRP)[:, None])
    needed = jnp.where(named, jax.random.randint(key_block, (DEVICES, N_GRP), 0, RB_DEV), -1).astype(jnp.int32)
    ranked = jnp.argsort(jnp.where(named, 0, 1).astype(jnp.int32) * N_GRP + groups[None, :], axis=1, stable=True).astype(jnp.int32)
    counted = jnp.sum(named.astype(jnp.int32), axis=1)
    picked = jax.random.randint(key_picked, (DEVICES, TF), 0, 1 << 20) % counted[:, None]
    far_list = jnp.take_along_axis(ranked, picked, axis=1).astype(jnp.int32)
    return (needed, far_list)


def draw_need_blocks(key, part):
    needed, far_list = linked_draw(key)
    return needed


def draw_far_groups(key, part):
    needed, far_list = linked_draw(key)
    return far_list


def set_ends(array, rng, smallest, largest):
    longest = array.shape.index(max(array.shape))
    spots = []
    for shift in (0, 1):
        where = [jax.random.randint(jax.random.fold_in(rng, axis), (), 0, length) for axis, length in enumerate(array.shape)]
        where[longest] = (where[longest] + shift) % array.shape[longest]
        spots.append(tuple(where))
    return array.at[spots[0]].set(smallest).at[spots[1]].set(largest)


def levels(rng, shape, pieces, least, largest):
    loudness = 1.0
    for dim, blocks in pieces:
        draws = jax.random.uniform(jax.random.fold_in(jax.random.fold_in(rng, 6), dim), (blocks,), jnp.float32, least / len(pieces), largest / len(pieces))
        loudness = loudness * jnp.repeat(jnp.exp(draws), shape[dim] // blocks).reshape((-1,) + (1,) * (len(shape) - 1 - dim))
    return loudness


def scatter_about(key, dims, scale, reach, pieces=(), kind=jnp.bfloat16):
    entries = scale * jax.random.normal(key, dims, jnp.float32)
    if pieces:
        entries = entries * levels(key, dims, pieces, -0.22, 0.18)
    return jnp.clip(entries, -reach, reach).astype(kind)


def setup_inputs(seed: int = 0) -> dict:
    key_list = jax.random.split(jax.random.key(seed), 7)
    tiles_near = scatter_about(key_list[0], (DEVICES * TN, TILE, TILE), (TILE * (N_BLK * NPS + FAR_RB)) ** -0.5, 0.078125, ((0, 256),))
    near_cols = set_ends(jax.random.randint(key_list[1], (DEVICES, TN), 0, RB_DEV), jax.random.fold_in(key_list[1], 1), 0, RB_DEV - 1).astype(jnp.int32)
    tiles_far = scatter_about(key_list[2], (DEVICES * TF, TILE, TILE), (TILE * (N_BLK * NPS + FAR_RB)) ** -0.5, 0.078125, ((0, 256),))
    far_groups = draw_far_groups(jax.random.fold_in(key_list[6], 71), 0)
    need_blocks = draw_need_blocks(jax.random.fold_in(key_list[6], 71), 0)
    start_vectors = scatter_about(key_list[5], (ROWS, K), 1.0, 6.0, ((0, 256),))
    return {"tiles_near": tiles_near, "near_cols": near_cols, "tiles_far": tiles_far, "far_groups": far_groups, "need_blocks": need_blocks, "start_vectors": start_vectors}


def reference(tiles_near, near_cols, tiles_far, far_groups, need_blocks, start_vectors):
    device_ids = jnp.arange(DEVICES, dtype=jnp.int32)
    near_all = tiles_near.reshape(DEVICES, RB_DEV, N_BLK * NPS, TILE, TILE)
    near_index = near_cols.reshape(DEVICES, RB_DEV, N_BLK * NPS)
    far_all = tiles_far.reshape(DEVICES, RB_DEV, FAR_RB, TILE, TILE)
    far_index = far_groups.reshape(DEVICES, RB_DEV, FAR_RB)
    source_pos = (jnp.arange(N_BLK * NPS, dtype=jnp.int32) // NPS).astype(jnp.int32)
    current = start_vectors
    vectors = start_vectors.astype(jnp.float32)
    for iteration in range(ITERS):
        block_table = current.reshape(NB, TILE, K)

        def one_device(inputs):
            device, near_tiles, near_ids, far_tiles, far_ids, needed = inputs
            group_id = device // N_BLK
            position = device % N_BLK
            near_block = ((group_id * N_BLK + source_pos)[None, :] * RB_DEV + near_ids).astype(jnp.int32)
            near_rows = block_table[near_block].astype(jnp.float32)
            near_part = jnp.einsum('rnij,rnjk->rik', near_tiles.astype(jnp.float32), near_rows)
            far_block = ((far_ids * N_BLK + position) * RB_DEV + needed[far_ids]).astype(jnp.int32)
            far_rows = block_table[far_block].astype(jnp.float32)
            far_part = jnp.einsum('rnij,rnjk->rik', far_tiles.astype(jnp.float32), far_rows)
            return near_part + far_part
        product = lax.map(one_device, (device_ids, near_all, near_index, far_all, far_index, need_blocks))
        flat_rows = product.reshape(ROWS, K)
        gram = jnp.dot(flat_rows.T.astype(jnp.float32), flat_rows.astype(jnp.float32), precision=lax.Precision.HIGHEST, preferred_element_type=jnp.float32) / ROWS
        factor = jnp.linalg.cholesky(gram)
        identity_matrix = jnp.eye(K, dtype=jnp.float32)
        inverse = lax.linalg.triangular_solve(factor, identity_matrix, left_side=True, lower=True).T
        vectors = jnp.dot(flat_rows.astype(jnp.float32), inverse.astype(jnp.float32), precision=lax.Precision.HIGHEST, preferred_element_type=jnp.float32)
        current = vectors.astype(jnp.bfloat16)
    return vectors
```

```python
import functools

import jax
import jax.numpy as jnp
from jax import lax
from jax.experimental import pallas as pl
from jax.experimental.pallas import tpu as pltpu
from jax.sharding import PartitionSpec as P

ITERS = 2
MESH = pl.DeviceIdType.MESH
NX, NY, NC, NZ = 4, 4, 2, 8
NG = NX * NY * NC
LINE = NC * NZ
PLANE = NX * NY


def wait_bytes(ref, sem):
    pltpu.make_async_copy(ref, ref, sem).wait()


def product_kernel(
    near_cols, far_groups, need, cur, tiles_near, tiles_far,
    product, gram_out,
    a_near, a_far, near_buf, far_buf, stage, request, wanted,
    gram, rs_buf, part, plane_buf, total, gathered,
    tile_sem, ring_send, ring_recv, req_send, req_recv, far_send, far_recv,
    ar_send, ar_recv,
):
    g = lax.axis_index("grp")
    z = lax.axis_index("blk")
    core = lax.rem(g, NC)
    xy = g // NC
    x, y = xy // NY, lax.rem(xy, NY)
    blocks = cur.shape[0]
    half = blocks // 2

    load_near = pltpu.make_async_copy(tiles_near, a_near, tile_sem.at[0])
    load_far = pltpu.make_async_copy(tiles_far, a_far, tile_sem.at[1])
    load_near.start()
    load_far.start()

    def group_peer(k):
        dc, dy, dx = lax.rem(k, NC), lax.rem(k // NC, NY), k // (NC * NY)
        px, py, pc = lax.rem(x + dx, NX), lax.rem(y + dy, NY), lax.rem(core + dc, NC)
        return (px * NY + py) * NC + pc

    def line_peer(k):
        pz, pc = lax.rem(z + k // NC, NZ), lax.rem(core + lax.rem(k, NC), NC)
        return xy * NC + pc, pz

    def plane_peer(k):
        px, py = lax.rem(x + k // NY, NX), lax.rem(y + lax.rem(k, NY), NY)
        return (px * NY + py) * NC + core

    barrier = pltpu.get_barrier_semaphore()

    def greet_group(k, carry):
        pl.semaphore_signal(barrier, inc=1, device_id=(group_peer(k), z), device_id_type=MESH)
        return carry

    def greet_line(k, carry):
        pl.semaphore_signal(barrier, inc=1, device_id=line_peer(k), device_id_type=MESH)
        return carry

    lax.fori_loop(1, NG, greet_group, 0)
    lax.fori_loop(NC, LINE, greet_line, 0)

    def fill_request(h, carry):
        request[h] = jnp.full(request.shape[1:], need[0, h], jnp.int32).astype(jnp.float32)
        return carry

    lax.fori_loop(0, NG, fill_request, 0)
    near_buf[z] = cur[...]
    far_buf[g] = cur[0]
    pl.semaphore_wait(barrier, NG - 1 + LINE - NC)

    right, left = lax.rem(z + 1, NZ), lax.rem(z + NZ - 1, NZ)

    def ring(direction, step, part_id):
        owner = lax.rem(z + (step if direction else NZ - step), NZ)
        rows = pl.ds(part_id * half, half)
        src = cur.at[rows] if step == 0 else near_buf.at[owner, rows]
        return pltpu.make_async_remote_copy(
            src_ref=src,
            dst_ref=near_buf.at[owner, rows],
            send_sem=ring_send.at[direction],
            recv_sem=ring_recv.at[direction, step, part_id],
            device_id=(g, left if direction else right),
            device_id_type=MESH,
        )

    def parts(direction, step):
        if step < NZ // 2 - 1:
            return (0, 1) if direction == 0 else (1, 0)
        return (direction,)

    for i in range(2):
        for direction in (0, 1):
            ring(direction, 0, parts(direction, 0)[i]).start()

    def request_copy(k):
        peer = group_peer(k)
        return pltpu.make_async_remote_copy(
            src_ref=request.at[peer],
            dst_ref=wanted.at[g],
            send_sem=req_send,
            recv_sem=req_recv,
            device_id=(peer, z),
            device_id_type=MESH,
        )

    def send_request(k, carry):
        request_copy(k).start()
        return carry

    lax.fori_loop(1, NG, send_request, 0)
    wait_bytes(wanted.at[pl.ds(0, NG - 1)], req_recv)

    def send_far(k, carry):
        peer = group_peer(k)
        choice = wanted[peer][None]
        picked = cur[0].astype(jnp.float32).reshape(-1, 8, 128)
        for b in range(1, blocks):
            other = cur[b].astype(jnp.float32).reshape(-1, 8, 128)
            picked = jnp.where(choice == float(b), other, picked)
        stage[peer] = picked.reshape(stage.shape[1:]).astype(stage.dtype)
        pltpu.make_async_remote_copy(
            src_ref=stage.at[peer],
            dst_ref=far_buf.at[g],
            send_sem=far_send,
            recv_sem=far_recv,
            device_id=(peer, z),
            device_id_type=MESH,
        ).start()
        return carry

    lax.fori_loop(1, NG, send_far, 0)

    for step in range(1, NZ // 2):
        for i in range(2):
            for direction in (0, 1):
                order = parts(direction, step - 1)
                here = order[i]
                ring(direction, step - 1, here).wait_recv()
                if here in parts(direction, step):
                    ring(direction, step, here).start()
    for direction in (0, 1):
        ring(direction, NZ // 2 - 1, direction).wait_recv()

    load_near.wait()
    per_row = a_near.shape[0] // blocks
    per_source = per_row // NZ
    far_row = a_far.shape[0] // blocks
    tile = cur.shape[1]

    def near_rows(r, carry):
        acc = jnp.zeros((tile, cur.shape[2]), jnp.float32)
        for j in range(per_row):
            t = r * per_row + j
            acc += jnp.dot(
                a_near[t], near_buf[j // per_source, near_cols[0, t]],
                preferred_element_type=jnp.float32,
            )
        product[pl.ds(r * tile, tile), :] = acc
        return carry

    lax.fori_loop(0, blocks, near_rows, 0)

    load_far.wait()
    wait_bytes(far_buf.at[pl.ds(0, NG - 1)], far_recv)

    def far_rows(r, carry):
        rows = pl.ds(r * tile, tile)
        acc = product[rows, :]
        for j in range(far_row):
            t = r * far_row + j
            acc += jnp.dot(
                a_far[t], far_buf[far_groups[0, t]], preferred_element_type=jnp.float32
            )
        product[rows, :] = acc
        return carry

    lax.fori_loop(0, blocks, far_rows, 0)

    flat = product[...]
    gram[...] = lax.dot_general(
        flat, flat, (((0,), (0,)), ((), ())),
        precision=lax.Precision.HIGHEST, preferred_element_type=jnp.float32,
    ).reshape(gram.shape)

    q = z * NC + core

    def scatter(k, carry):
        pg, pz = line_peer(k)
        pq = pz * NC + lax.rem(pg, NC)
        pltpu.make_async_remote_copy(
            src_ref=gram.at[pq], dst_ref=rs_buf.at[q],
            send_sem=ar_send.at[0], recv_sem=ar_recv.at[0],
            device_id=(pg, pz), device_id_type=MESH,
        ).start()
        return carry

    lax.fori_loop(1, LINE, scatter, 0)
    rs_buf[q] = gram[q]
    wait_bytes(rs_buf.at[pl.ds(0, LINE - 1)], ar_recv.at[0])
    part[...] = jnp.sum(rs_buf[...], axis=0)
    plane_buf[xy] = part[...]

    def spread(k, carry):
        pltpu.make_async_remote_copy(
            src_ref=part, dst_ref=plane_buf.at[xy],
            send_sem=ar_send.at[1], recv_sem=ar_recv.at[1],
            device_id=(plane_peer(k), z), device_id_type=MESH,
        ).start()
        return carry

    lax.fori_loop(1, PLANE, spread, 0)
    wait_bytes(plane_buf.at[pl.ds(0, PLANE - 1)], ar_recv.at[1])
    total[...] = jnp.sum(plane_buf[...], axis=0)
    gathered[q] = total[...]

    def collect(k, carry):
        pltpu.make_async_remote_copy(
            src_ref=total, dst_ref=gathered.at[q],
            send_sem=ar_send.at[2], recv_sem=ar_recv.at[2],
            device_id=line_peer(k), device_id_type=MESH,
        ).start()
        return carry

    lax.fori_loop(1, LINE, collect, 0)
    wait_bytes(gathered.at[pl.ds(0, LINE - 1)], ar_recv.at[2])
    gram_out[...] = gathered[...].reshape(gram_out.shape)

    sent = NZ // 2 * blocks - half
    for direction in (0, 1):
        wait_bytes(far_buf.at[pl.ds(0, sent)], ring_send.at[direction])
    wait_bytes(request.at[pl.ds(0, NG - 1)], req_send)
    wait_bytes(stage.at[pl.ds(0, NG - 1)], far_send)
    wait_bytes(rs_buf.at[pl.ds(0, LINE - 1)], ar_send.at[0])
    wait_bytes(plane_buf.at[pl.ds(0, PLANE - 1)], ar_send.at[1])
    wait_bytes(gathered.at[pl.ds(0, LINE - 1)], ar_send.at[2])


def product_and_gram(near_cols, far_groups, need, cur, tiles_near, tiles_far):
    blocks, tile, width = cur.shape
    rows = width // LINE
    return pl.pallas_call(
        product_kernel,
        out_shape=(
            jax.ShapeDtypeStruct((blocks * tile, width), jnp.float32),
            jax.ShapeDtypeStruct((width, width), jnp.float32),
        ),
        in_specs=[pl.BlockSpec(memory_space=pltpu.SMEM)] * 3
        + [pl.BlockSpec(memory_space=pltpu.VMEM)]
        + [pl.BlockSpec(memory_space=pl.ANY)] * 2,
        out_specs=(pl.BlockSpec(memory_space=pltpu.VMEM),) * 2,
        scratch_shapes=[
            pltpu.VMEM(tiles_near.shape, tiles_near.dtype),
            pltpu.VMEM(tiles_far.shape, tiles_far.dtype),
            pltpu.VMEM((NZ, blocks, tile, width), cur.dtype),
            pltpu.VMEM((NG, tile, width), cur.dtype),
            pltpu.VMEM((NG, tile, width), cur.dtype),
            pltpu.VMEM((NG, 8, 128), jnp.float32),
            pltpu.VMEM((NG, 8, 128), jnp.float32),
            pltpu.VMEM((LINE, rows, width), jnp.float32),
            pltpu.VMEM((LINE, rows, width), jnp.float32),
            pltpu.VMEM((rows, width), jnp.float32),
            pltpu.VMEM((PLANE, rows, width), jnp.float32),
            pltpu.VMEM((rows, width), jnp.float32),
            pltpu.VMEM((LINE, rows, width), jnp.float32),
            pltpu.SemaphoreType.DMA((2,)),
            pltpu.SemaphoreType.DMA((2,)),
            pltpu.SemaphoreType.DMA((2, NZ // 2, 2)),
            pltpu.SemaphoreType.DMA,
            pltpu.SemaphoreType.DMA,
            pltpu.SemaphoreType.DMA,
            pltpu.SemaphoreType.DMA,
            pltpu.SemaphoreType.DMA((3,)),
            pltpu.SemaphoreType.DMA((3,)),
        ],
        compiler_params=pltpu.CompilerParams(
            collective_id=0, has_side_effects=True, vmem_limit_bytes=40 << 20
        ),
        name="product_and_gram",
    )(near_cols, far_groups, need, cur, tiles_near, tiles_far)


def per_device(tiles_near, near_cols, tiles_far, far_groups, need_blocks, start_vectors):
    tile_size = tiles_near.shape[1]
    rows, vec_width = start_vectors.shape
    blocks = rows // tile_size
    total_rows = rows * lax.axis_size("blk") * lax.axis_size("grp")
    current = start_vectors
    for iteration in range(ITERS):
        local_rows = current.reshape(blocks, tile_size, vec_width)
        flat_rows, gram = product_and_gram(
            near_cols, far_groups, need_blocks, local_rows, tiles_near, tiles_far
        )
        gram = gram / total_rows
        factor = jnp.linalg.cholesky(gram)
        identity_matrix = jnp.eye(vec_width, dtype=jnp.float32)
        inverse = lax.linalg.triangular_solve(factor, identity_matrix, left_side=True, lower=True).T
        vectors = jnp.dot(
            flat_rows, inverse, precision=lax.Precision.HIGHEST, preferred_element_type=jnp.float32
        )
        current = vectors.astype(jnp.bfloat16)
    return vectors


def solution(mesh):
    in_specs = (
        P(("grp", "blk"), None, None),
        P(("grp", "blk"), None),
        P(("grp", "blk"), None, None),
        P(("grp", "blk"), None),
        P(("grp", "blk"), None),
        P(("grp", "blk"), None),
    )
    out_specs = P(("grp", "blk"), None)
    return jax.shard_map(
        per_device, mesh=mesh, in_specs=in_specs, out_specs=out_specs, check_vma=False
    )
```

```python
import jax
import jax.numpy as jnp
from jax import lax
from jax.experimental import pallas as pl
from jax.experimental.pallas import tpu as pltpu
from jax.sharding import PartitionSpec as P

ITERS = 2
MESH = pl.DeviceIdType.MESH
NX, NY, NC, NZ = 4, 4, 2, 8
NG = NX * NY * NC
LINE = NC * NZ
PLANE = NX * NY
PANEL = 8
STEP_BUFFERS = NZ + 6


def wait_bytes(ref, sem):
    pltpu.make_async_copy(ref, ref, sem).wait()


def inverse_factor(gram, work, out):
    n = gram.shape[0]
    row_id = lax.broadcasted_iota(jnp.int32, (n, n), 0)
    col_id = lax.broadcasted_iota(jnp.int32, (n, n), 1)
    work[:, :n] = gram
    work[:, n:] = (row_id == col_id).astype(jnp.float32)
    lane = lax.broadcasted_iota(jnp.int32, (PANEL, n), 1)
    sub = lax.broadcasted_iota(jnp.int32, (PANEL, 2 * n), 0)

    def panel(p, first):
        start = pl.multiple_of(p * PANEL, PANEL)
        top = work[pl.ds(start, PANEL), :]
        diag = pltpu.roll(top[:, :n], lax.rem(n - start, n), 1)
        a, low, solved = {}, {}, []
        for j in range(PANEL):
            for i in range(j, PANEL):
                a[i, j] = jnp.broadcast_to(diag[i : i + 1, j : j + 1], (PANEL, n))
        for j in range(PANEL):
            scale = lax.rsqrt(a[j, j])
            row = jnp.broadcast_to(top[j : j + 1, :], (PANEL, 2 * n))
            for k in range(j):
                row = row - jnp.concatenate([low[j, k]] * 2, 1) * solved[k]
            solved.append(row * jnp.concatenate([scale] * 2, 1))
            for i in range(j + 1, PANEL):
                low[i, j] = a[i, j] * scale
            for k in range(j + 1, PANEL):
                for i in range(k, PANEL):
                    a[i, k] = a[i, k] - low[i, j] * low[k, j]
        block = solved[0]
        for j in range(1, PANEL):
            block = jnp.where(sub == j, solved[j], block)
        out[pl.ds(start, PANEL), :] = block[:, n:]
        left = jnp.where(lane >= start + PANEL, block[:, :n], 0.0)
        columns = left.T[first:].reshape((n - first) // PANEL, PANEL, PANEL)
        rows = pl.ds(first, n - first)
        rest = work[rows, :].reshape((n - first) // PANEL, PANEL, 2 * n)
        for j in range(PANEL):
            rest = rest - columns[:, :, j : j + 1] * solved[j][None]
        work[rows, :] = rest.reshape(n - first, 2 * n)

    def first_half(p, carry):
        panel(p, 0)
        return carry

    def second_half(p, carry):
        panel(p, n // 2)
        return carry

    steps = n // PANEL
    lax.fori_loop(0, steps // 2, first_half, 0)
    lax.fori_loop(steps // 2, steps, second_half, 0)


def iteration_kernel(*refs):
    (near_cols, far_groups, need, start, tiles_near, tiles_far, vectors_out,
     a_near, a_far, stage, request, wanted, product, gram, work, inverse) = refs[:16]
    refs = refs[16:]
    per_step = [refs[i * STEP_BUFFERS : (i + 1) * STEP_BUFFERS] for i in range(ITERS)]
    (tile_sem, ring_send, ring_recv, req_send, req_recv, far_send, far_recv,
     ar_send, ar_recv) = refs[ITERS * STEP_BUFFERS :]

    g = lax.axis_index("grp")
    z = lax.axis_index("blk")
    core = lax.rem(g, NC)
    xy = g // NC
    x, y = xy // NY, lax.rem(xy, NY)
    blocks, tile, width = start.shape
    half = blocks // 2
    rows_each = width // LINE
    q = z * NC + core

    load_near = pltpu.make_async_copy(tiles_near, a_near, tile_sem.at[0])
    load_far = pltpu.make_async_copy(tiles_far, a_far, tile_sem.at[1])
    load_near.start()
    load_far.start()

    def group_peer(k):
        dc, dy, dx = lax.rem(k, NC), lax.rem(k // NC, NY), k // (NC * NY)
        px, py, pc = lax.rem(x + dx, NX), lax.rem(y + dy, NY), lax.rem(core + dc, NC)
        return (px * NY + py) * NC + pc

    def line_peer(k):
        pz, pc = lax.rem(z + k // NC, NZ), lax.rem(core + lax.rem(k, NC), NC)
        return xy * NC + pc, pz

    def plane_peer(k):
        px, py = lax.rem(x + k // NY, NX), lax.rem(y + lax.rem(k, NY), NY)
        return (px * NY + py) * NC + core

    barrier = pltpu.get_barrier_semaphore()

    def greet_group(k, carry):
        pl.semaphore_signal(barrier, inc=1, device_id=(group_peer(k), z), device_id_type=MESH)
        return carry

    def greet_line(k, carry):
        pl.semaphore_signal(barrier, inc=1, device_id=line_peer(k), device_id_type=MESH)
        return carry

    lax.fori_loop(1, NG, greet_group, 0)
    lax.fori_loop(NC, LINE, greet_line, 0)

    def fill_request(h, carry):
        request[h] = jnp.full(request.shape[1:], need[0, h], jnp.int32).astype(jnp.float32)
        return carry

    lax.fori_loop(0, NG, fill_request, 0)
    per_step[0][0][...] = start[...]
    pl.semaphore_wait(barrier, NG - 1 + LINE - NC)

    right, left = lax.rem(z + 1, NZ), lax.rem(z + NZ - 1, NZ)
    last = NZ // 2 - 1

    def parts(direction, step):
        if step < last:
            return (0, 1) if direction == 0 else (1, 0)
        return (direction,)

    def send_request(k, carry):
        peer = group_peer(k)
        pltpu.make_async_remote_copy(
            src_ref=request.at[peer], dst_ref=wanted.at[g],
            send_sem=req_send, recv_sem=req_recv,
            device_id=(peer, z), device_id_type=MESH,
        ).start()
        return carry

    near_row = a_near.shape[0] // blocks
    per_source = near_row // NZ
    far_row = a_far.shape[0] // blocks

    for it in range(ITERS):
        own, away = per_step[it][0], per_step[it][1 : NZ]
        far_buf, rs_buf, part, plane_buf, total, gathered = per_step[it][NZ:]

        def slot(direction, step):
            return away[2 * last] if step == last else away[2 * step + direction]

        def ring(direction, step, part_id):
            rows = pl.ds(part_id * half, half)
            src = own if step == 0 else slot(direction, step - 1)
            return pltpu.make_async_remote_copy(
                src_ref=src.at[rows],
                dst_ref=slot(direction, step).at[rows],
                send_sem=ring_send.at[direction],
                recv_sem=ring_recv.at[it, direction, step, part_id],
                device_id=(g, left if direction else right),
                device_id_type=MESH,
            )

        for i in range(2):
            for direction in (0, 1):
                ring(direction, 0, parts(direction, 0)[i]).start()

        if it == 0:
            lax.fori_loop(1, NG, send_request, 0)
        far_buf[g] = own[0]
        if it == 0:
            wait_bytes(wanted.at[pl.ds(0, NG - 1)], req_recv)

        def send_far(k, carry):
            peer = group_peer(k)
            choice = wanted[peer][None]
            picked = own[0].astype(jnp.float32).reshape(-1, 8, 128)
            for b in range(1, blocks):
                other = own[b].astype(jnp.float32).reshape(-1, 8, 128)
                picked = jnp.where(choice == float(b), other, picked)
            stage[peer] = picked.reshape(stage.shape[1:]).astype(stage.dtype)
            pltpu.make_async_remote_copy(
                src_ref=stage.at[peer], dst_ref=far_buf.at[g],
                send_sem=far_send, recv_sem=far_recv.at[it],
                device_id=(peer, z), device_id_type=MESH,
            ).start()
            return carry

        lax.fori_loop(1, NG, send_far, 0)

        def near_part(shard, source, first):
            def one_row(r, carry):
                rows = pl.ds(pl.multiple_of(r * tile, tile), tile)
                acc = None if first else product[rows, :]
                for n in range(per_source):
                    t = r * near_row + source * per_source + n
                    term = jnp.dot(
                        a_near[t], shard[near_cols[0, t]], preferred_element_type=jnp.float32
                    )
                    acc = term if acc is None else acc + term
                product[rows, :] = acc
                return carry

            lax.fori_loop(0, blocks, one_row, 0)

        if it == 0:
            load_near.wait()
            load_far.wait()
        near_part(own, z, True)
        for step in range(NZ // 2):
            for i in range(2):
                for direction in (0, 1):
                    if i < len(parts(direction, step)):
                        here = parts(direction, step)[i]
                        ring(direction, step, here).wait_recv()
                        if step < last and here in parts(direction, step + 1):
                            ring(direction, step + 1, here).start()
            if step < last:
                near_part(slot(0, step), lax.rem(z + NZ - 1 - step, NZ), False)
                near_part(slot(1, step), lax.rem(z + 1 + step, NZ), False)
            else:
                near_part(slot(0, step), lax.rem(z + NZ // 2, NZ), False)

        wait_bytes(far_buf.at[pl.ds(0, NG - 1)], far_recv.at[it])

        def far_rows(r, carry):
            rows = pl.ds(pl.multiple_of(r * tile, tile), tile)
            acc = product[rows, :]
            for j in range(far_row):
                t = r * far_row + j
                acc += jnp.dot(
                    a_far[t], far_buf[far_groups[0, t]], preferred_element_type=jnp.float32
                )
            product[rows, :] = acc
            return carry

        lax.fori_loop(0, blocks, far_rows, 0)

        flat = product[...]
        gram[...] = lax.dot_general(
            flat, flat, (((0,), (0,)), ((), ())),
            precision=lax.Precision.HIGHEST, preferred_element_type=jnp.float32,
        ).reshape(gram.shape)

        def scatter(k, carry):
            pg, pz = line_peer(k)
            pltpu.make_async_remote_copy(
                src_ref=gram.at[pz * NC + lax.rem(pg, NC)], dst_ref=rs_buf.at[q],
                send_sem=ar_send.at[0], recv_sem=ar_recv.at[it, 0],
                device_id=(pg, pz), device_id_type=MESH,
            ).start()
            return carry

        lax.fori_loop(1, LINE, scatter, 0)
        rs_buf[q] = gram[q]
        wait_bytes(rs_buf.at[pl.ds(0, LINE - 1)], ar_recv.at[it, 0])
        part[...] = jnp.sum(rs_buf[...], axis=0)
        plane_buf[xy] = part[...]

        def spread(k, carry):
            pltpu.make_async_remote_copy(
                src_ref=part, dst_ref=plane_buf.at[xy],
                send_sem=ar_send.at[1], recv_sem=ar_recv.at[it, 1],
                device_id=(plane_peer(k), z), device_id_type=MESH,
            ).start()
            return carry

        lax.fori_loop(1, PLANE, spread, 0)
        wait_bytes(plane_buf.at[pl.ds(0, PLANE - 1)], ar_recv.at[it, 1])
        total[...] = jnp.sum(plane_buf[...], axis=0)
        gathered[q] = total[...]

        def collect(k, carry):
            pltpu.make_async_remote_copy(
                src_ref=total, dst_ref=gathered.at[q],
                send_sem=ar_send.at[2], recv_sem=ar_recv.at[it, 2],
                device_id=line_peer(k), device_id_type=MESH,
            ).start()
            return carry

        lax.fori_loop(1, LINE, collect, 0)
        wait_bytes(gathered.at[pl.ds(0, LINE - 1)], ar_recv.at[it, 2])

        sent = (last + 1) * blocks - half
        for direction in (0, 1):
            wait_bytes(far_buf.at[pl.ds(0, sent)], ring_send.at[direction])
        if it == 0:
            wait_bytes(request.at[pl.ds(0, NG - 1)], req_send)
        wait_bytes(stage.at[pl.ds(0, NG - 1)], far_send)
        wait_bytes(rs_buf.at[pl.ds(0, LINE - 1)], ar_send.at[0])
        wait_bytes(plane_buf.at[pl.ds(0, PLANE - 1)], ar_send.at[1])
        wait_bytes(gathered.at[pl.ds(0, LINE - 1)], ar_send.at[2])

        total_rows = float(blocks * tile * NG * NZ)
        inverse_factor(gathered[...].reshape(width, width) / total_rows, work, inverse)

        def make_vectors(r, carry):
            rows = pl.ds(pl.multiple_of(r * tile, tile), tile)
            block = lax.dot_general(
                product[rows, :], inverse[...], (((1,), (1,)), ((), ())),
                precision=lax.Precision.HIGHEST, preferred_element_type=jnp.float32,
            )
            if it == ITERS - 1:
                vectors_out[rows, :] = block
            else:
                per_step[it + 1][0][r] = block.astype(start.dtype)
            return carry

        lax.fori_loop(0, blocks, make_vectors, 0)


def iterate(near_cols, far_groups, need, start, tiles_near, tiles_far):
    blocks, tile, width = start.shape
    rows = width // LINE
    step_buffers = (
        [pltpu.VMEM((blocks, tile, width), start.dtype)] * NZ
        + [
            pltpu.VMEM((NG, tile, width), start.dtype),
            pltpu.VMEM((LINE, rows, width), jnp.float32),
            pltpu.VMEM((rows, width), jnp.float32),
            pltpu.VMEM((PLANE, rows, width), jnp.float32),
            pltpu.VMEM((rows, width), jnp.float32),
            pltpu.VMEM((LINE, rows, width), jnp.float32),
        ]
    )
    assert len(step_buffers) == STEP_BUFFERS
    return pl.pallas_call(
        iteration_kernel,
        out_shape=jax.ShapeDtypeStruct((blocks * tile, width), jnp.float32),
        in_specs=[pl.BlockSpec(memory_space=pltpu.SMEM)] * 3
        + [pl.BlockSpec(memory_space=pltpu.VMEM)]
        + [pl.BlockSpec(memory_space=pltpu.HBM)] * 2,
        out_specs=pl.BlockSpec(memory_space=pltpu.VMEM),
        scratch_shapes=[
            pltpu.VMEM(tiles_near.shape, tiles_near.dtype),
            pltpu.VMEM(tiles_far.shape, tiles_far.dtype),
            pltpu.VMEM((NG, tile, width), start.dtype),
            pltpu.VMEM((NG, 8, 128), jnp.float32),
            pltpu.VMEM((NG, 8, 128), jnp.float32),
            pltpu.VMEM((blocks * tile, width), jnp.float32),
            pltpu.VMEM((LINE, rows, width), jnp.float32),
            pltpu.VMEM((width, 2 * width), jnp.float32),
            pltpu.VMEM((width, width), jnp.float32),
        ]
        + step_buffers * ITERS
        + [
            pltpu.SemaphoreType.DMA((2,)),
            pltpu.SemaphoreType.DMA((2,)),
            pltpu.SemaphoreType.DMA((ITERS, 2, NZ // 2, 2)),
            pltpu.SemaphoreType.DMA,
            pltpu.SemaphoreType.DMA,
            pltpu.SemaphoreType.DMA,
            pltpu.SemaphoreType.DMA((ITERS,)),
            pltpu.SemaphoreType.DMA((3,)),
            pltpu.SemaphoreType.DMA((ITERS, 3)),
        ],
        compiler_params=pltpu.CompilerParams(
            collective_id=0, has_side_effects=True, vmem_limit_bytes=48 << 20
        ),
        name="iterate",
    )(near_cols, far_groups, need, start, tiles_near, tiles_far)


def per_device(tiles_near, near_cols, tiles_far, far_groups, need_blocks, start_vectors):
    tile_size = tiles_near.shape[1]
    rows, vec_width = start_vectors.shape
    start = start_vectors.reshape(rows // tile_size, tile_size, vec_width)
    return iterate(near_cols, far_groups, need_blocks, start, tiles_near, tiles_far)


def solution(mesh):
    in_specs = (
        P(("grp", "blk"), None, None),
        P(("grp", "blk"), None),
        P(("grp", "blk"), None, None),
        P(("grp", "blk"), None),
        P(("grp", "blk"), None),
        P(("grp", "blk"), None),
    )
    out_specs = P(("grp", "blk"), None)
    return jax.shard_map(
        per_device, mesh=mesh, in_specs=in_specs, out_specs=out_specs, check_vma=False
    )
```

```python
import jax
import jax.numpy as jnp
from jax import lax
from jax.experimental import pallas as pl
from jax.experimental.pallas import tpu as pltpu
from jax.sharding import PartitionSpec as P

ITERS = 2
MESH = pl.DeviceIdType.MESH
NX, NY, NC, NZ = 4, 4, 2, 8
NG = NX * NY * NC
LINE = NC * NZ
PLANE = NX * NY
PANEL = 16
SIDE = NX
STEP_BUFFERS = NZ + SIDE - 1 + 6
FAR_IN = SIDE * (NC * SIDE - 1)


def wait_bytes(ref, sem):
    pltpu.make_async_copy(ref, ref, sem).wait()


def split(value):
    high = value.astype(jnp.bfloat16)
    rest = value - high.astype(jnp.float32)
    middle = rest.astype(jnp.bfloat16)
    return high, middle, (rest - middle.astype(jnp.float32)).astype(jnp.bfloat16)


def inverse_factor(gram, work, out):
    n = gram.shape[0]
    row_id = lax.broadcasted_iota(jnp.int32, (n, n), 0)
    col_id = lax.broadcasted_iota(jnp.int32, (n, n), 1)
    work[:, :n] = gram
    work[:, n:] = (row_id == col_id).astype(jnp.float32)
    sub = lax.broadcasted_iota(jnp.int32, (8, 2 * n), 0)

    def wide(value):
        return jnp.concatenate([value] * 2, 1)

    def panel(p, carry):
        start = pl.multiple_of(p * PANEL, PANEL)
        rows = pl.ds(start, PANEL)
        top = work[rows, :]
        diag = pltpu.roll(top[:, :n], lax.rem(n - start, n), 1)
        a, low, scale, solved = {}, {}, [], []
        for j in range(PANEL):
            for i in range(j, PANEL):
                a[i, j] = jnp.broadcast_to(diag[i : i + 1, j : j + 1], (8, n))
        for j in range(PANEL):
            scale.append(lax.rsqrt(a[j, j]))
            for i in range(j + 1, PANEL):
                low[i, j] = a[i, j] * scale[j]
            for k in range(j + 1, PANEL):
                for i in range(k, PANEL):
                    a[i, k] = a[i, k] - low[i, j] * low[k, j]
        for j in range(PANEL):
            row = jnp.broadcast_to(top[j : j + 1, :], (8, 2 * n))
            for k in range(j):
                row = row - wide(low[j, k]) * solved[k]
            solved.append(row * wide(scale[j]))
        pieces = []
        for b in range(0, PANEL, 8):
            piece = solved[b]
            for j in range(1, 8):
                piece = jnp.where(sub == j, solved[b + j], piece)
            pieces.append(piece)
        block = jnp.concatenate(pieces, 0)
        out[rows, :] = block[:, n:]
        high, middle, small = split(block)
        left = jnp.concatenate([v[:, :n] for v in (high, high, middle, high, small, middle)], 0)
        right = jnp.concatenate([high, middle, high, small, high, middle], 0)
        work[...] = work[...] - lax.dot_general(
            left, right, (((0,), (0,)), ((), ())), preferred_element_type=jnp.float32
        )
        return carry

    lax.fori_loop(0, n // PANEL, panel, 0)


def iteration_kernel(*refs):
    (near_cols, far_groups, need, start, tiles_near, tiles_far, vectors_out,
     a_near, a_far, stage, request, wanted, product, gram, work, inverse) = refs[:16]
    refs = refs[16:]
    per_step = [refs[i * STEP_BUFFERS : (i + 1) * STEP_BUFFERS] for i in range(ITERS)]
    (tile_sem, ring_send, ring_recv, req_send, req_recv, share_send, share_recv, far_send, far_recv,
     ar_send, ar_recv) = refs[ITERS * STEP_BUFFERS :]

    g = lax.axis_index("grp")
    z = lax.axis_index("blk")
    core = lax.rem(g, NC)
    xy = g // NC
    x, y = xy // NY, lax.rem(xy, NY)
    blocks, tile, width = start.shape
    half = blocks // 2
    rows_each = width // LINE
    q = z * NC + core

    load_near = pltpu.make_async_copy(tiles_near, a_near, tile_sem.at[0])
    load_far = pltpu.make_async_copy(tiles_far, a_far, tile_sem.at[1])
    load_near.start()
    load_far.start()

    def group_peer(k):
        dc, dy, dx = lax.rem(k, NC), lax.rem(k // NC, NY), k // (NC * NY)
        px, py, pc = lax.rem(x + dx, NX), lax.rem(y + dy, NY), lax.rem(core + dc, NC)
        return (px * NY + py) * NC + pc

    def group_at(first, second, which):
        px = first + which * (second - first)
        py = second + which * (first - second)
        return px * NY + py

    axis_a = x + core * (y - x)
    axis_b = y + core * (x - y)

    def same_core(first, second):
        return group_at(first, second, core) * NC + core

    def line_peer(k):
        pz, pc = lax.rem(z + k // NC, NZ), lax.rem(core + lax.rem(k, NC), NC)
        return xy * NC + pc, pz

    def plane_peer(k):
        px, py = lax.rem(x + k // NY, NX), lax.rem(y + lax.rem(k, NY), NY)
        return (px * NY + py) * NC + core

    barrier = pltpu.get_barrier_semaphore()

    def greet_group(k, carry):
        pl.semaphore_signal(barrier, inc=1, device_id=(group_peer(k), z), device_id_type=MESH)
        return carry

    def greet_line(k, carry):
        pl.semaphore_signal(barrier, inc=1, device_id=line_peer(k), device_id_type=MESH)
        return carry

    lax.fori_loop(1, NG, greet_group, 0)
    lax.fori_loop(NC, LINE, greet_line, 0)

    def fill_request(k, carry):
        t, b, a = k // (SIDE * SIDE), lax.rem(k // SIDE, SIDE), lax.rem(k, SIDE)
        source = group_at(a, b, t) * NC + t
        value = jnp.full(request.shape[3:], need[0, source], jnp.int32).astype(jnp.float32)
        request[t, b, a] = value
        return carry

    lax.fori_loop(0, NG, fill_request, 0)
    wanted[axis_b * NC + core] = request[core, axis_b]
    per_step[0][0][...] = start[...]
    pl.semaphore_wait(barrier, NG - 1 + LINE - NC)

    right, left = lax.rem(z + 1, NZ), lax.rem(z + NZ - 1, NZ)
    last = NZ // 2 - 1

    def parts(direction, step):
        if step < last:
            return (0, 1) if direction == 0 else (1, 0)
        return (direction,)

    def send_request(k, carry):
        t = lax.rem(core + k // SIDE, NC)
        mine_a, mine_b = x + t * (y - x), y + t * (x - y)
        b = lax.rem(mine_b + lax.rem(k, SIDE), SIDE)
        relay = group_at(mine_a, b, t) * NC + t
        pltpu.make_async_remote_copy(
            src_ref=request.at[t, b], dst_ref=wanted.at[mine_b * NC + core],
            send_sem=req_send, recv_sem=req_recv,
            device_id=(relay, z), device_id_type=MESH,
        ).start()
        return carry

    near_row = a_near.shape[0] // blocks
    per_source = near_row // NZ
    far_row = a_far.shape[0] // blocks

    for it in range(ITERS):
        own, away = per_step[it][0], per_step[it][1 : NZ]
        relay_buf = per_step[it][NZ : NZ + SIDE - 1]
        far_buf, rs_buf, part, plane_buf, total, gathered = per_step[it][NZ + SIDE - 1 :]

        def slot(direction, step):
            return away[2 * last] if step == last else away[2 * step + direction]

        def ring(direction, step, part_id):
            rows = pl.ds(part_id * half, half)
            src = own if step == 0 else slot(direction, step - 1)
            return pltpu.make_async_remote_copy(
                src_ref=src.at[rows],
                dst_ref=slot(direction, step).at[rows],
                send_sem=ring_send.at[direction],
                recv_sem=ring_recv.at[it, direction, step, part_id],
                device_id=(g, left if direction else right),
                device_id_type=MESH,
            )

        for i in range(2):
            for direction in (0, 1):
                ring(direction, 0, parts(direction, 0)[i]).start()

        if it == 0:
            lax.fori_loop(1, 2 * SIDE, send_request, 0)

        def share(k):
            return pltpu.make_async_remote_copy(
                src_ref=own, dst_ref=relay_buf[SIDE - k - 1],
                send_sem=share_send, recv_sem=share_recv.at[it, SIDE - k - 1],
                device_id=(same_core(lax.rem(axis_a + k, SIDE), axis_b), z), device_id_type=MESH,
            )

        for k in (1, 3, 2):
            share(k).start()
        if it == 0:
            wait_bytes(wanted.at[pl.ds(0, NC * SIDE - 1)], req_recv)

        def choose(shard, ask):
            choice = ask[None]
            picked = shard[0].astype(jnp.float32).reshape(-1, 8, 128)
            for b in range(1, blocks):
                other = shard[b].astype(jnp.float32).reshape(-1, 8, 128)
                picked = jnp.where(choice == float(b), other, picked)
            return picked.reshape(tile, width).astype(start.dtype)

        def pass_on(away_by):
            shard = own if away_by == 0 else relay_buf[away_by - 1]
            a = lax.rem(axis_a + away_by, SIDE)
            source = same_core(a, axis_b)

            def send_one(m, carry):
                b, c = lax.rem(axis_b + m // NC, SIDE), lax.rem(core + lax.rem(m, NC), NC)
                spot = away_by * (NC * SIDE - 1) + m - 1
                stage[spot] = choose(shard, wanted[b * NC + c, a])
                pltpu.make_async_remote_copy(
                    src_ref=stage.at[spot], dst_ref=far_buf.at[source],
                    send_sem=far_send, recv_sem=far_recv.at[it],
                    device_id=(group_at(axis_a, b, core) * NC + c, z), device_id_type=MESH,
                ).start()
                return carry

            lax.fori_loop(1, NC * SIDE, send_one, 0)
            far_buf[source] = choose(shard, wanted[axis_b * NC + core, a])

        pass_on(0)

        def near_part(shard, source, first):
            def one_row(r, carry):
                rows = pl.ds(pl.multiple_of(r * tile, tile), tile)
                acc = None if first else product[rows, :]
                for n in range(per_source):
                    t = r * near_row + source * per_source + n
                    term = jnp.dot(
                        a_near[t], shard[near_cols[0, t]], preferred_element_type=jnp.float32
                    )
                    acc = term if acc is None else acc + term
                product[rows, :] = acc
                return carry

            lax.fori_loop(0, blocks, one_row, 0)

        if it == 0:
            load_near.wait()
            load_far.wait()
        for step in range(NZ // 2):
            for i in range(2):
                for direction in (0, 1):
                    if i < len(parts(direction, step)):
                        here = parts(direction, step)[i]
                        ring(direction, step, here).wait_recv()
                        if step < last and here in parts(direction, step + 1):
                            ring(direction, step + 1, here).start()
            if step == 0:
                near_part(own, z, True)
                for k in (1, 3, 2):
                    share(SIDE - k).wait_recv()
                    pass_on(k)
            if step < last:
                near_part(slot(0, step), lax.rem(z + NZ - 1 - step, NZ), False)
                near_part(slot(1, step), lax.rem(z + 1 + step, NZ), False)
            else:
                near_part(slot(0, step), lax.rem(z + NZ // 2, NZ), False)

        wait_bytes(far_buf.at[pl.ds(0, FAR_IN)], far_recv.at[it])

        def far_rows(r, carry):
            rows = pl.ds(pl.multiple_of(r * tile, tile), tile)
            acc = product[rows, :]
            for j in range(far_row):
                t = r * far_row + j
                acc += jnp.dot(
                    a_far[t], far_buf[far_groups[0, t]], preferred_element_type=jnp.float32
                )
            product[rows, :] = acc
            return carry

        lax.fori_loop(0, blocks, far_rows, 0)

        flat = product[...]
        gram[...] = lax.dot_general(
            flat, flat, (((0,), (0,)), ((), ())),
            precision=lax.Precision.HIGHEST, preferred_element_type=jnp.float32,
        ).reshape(gram.shape)

        def scatter(k, carry):
            pg, pz = line_peer(k)
            pltpu.make_async_remote_copy(
                src_ref=gram.at[pz * NC + lax.rem(pg, NC)], dst_ref=rs_buf.at[q],
                send_sem=ar_send.at[0], recv_sem=ar_recv.at[it, 0],
                device_id=(pg, pz), device_id_type=MESH,
            ).start()
            return carry

        lax.fori_loop(1, LINE, scatter, 0)
        rs_buf[q] = gram[q]
        wait_bytes(rs_buf.at[pl.ds(0, LINE - 1)], ar_recv.at[it, 0])
        part[...] = jnp.sum(rs_buf[...], axis=0)
        plane_buf[xy] = part[...]

        def spread(k, carry):
            pltpu.make_async_remote_copy(
                src_ref=part, dst_ref=plane_buf.at[xy],
                send_sem=ar_send.at[1], recv_sem=ar_recv.at[it, 1],
                device_id=(plane_peer(k), z), device_id_type=MESH,
            ).start()
            return carry

        lax.fori_loop(1, PLANE, spread, 0)
        wait_bytes(plane_buf.at[pl.ds(0, PLANE - 1)], ar_recv.at[it, 1])
        total[...] = jnp.sum(plane_buf[...], axis=0)
        gathered[q] = total[...]

        def collect(k, carry):
            pltpu.make_async_remote_copy(
                src_ref=total, dst_ref=gathered.at[q],
                send_sem=ar_send.at[2], recv_sem=ar_recv.at[it, 2],
                device_id=line_peer(k), device_id_type=MESH,
            ).start()
            return carry

        lax.fori_loop(1, LINE, collect, 0)
        wait_bytes(gathered.at[pl.ds(0, LINE - 1)], ar_recv.at[it, 2])

        sent = (last + 1) * blocks - half
        for direction in (0, 1):
            wait_bytes(far_buf.at[pl.ds(0, sent)], ring_send.at[direction])
        if it == 0:
            wait_bytes(wanted.at[pl.ds(0, NC * SIDE - 1)], req_send)
        wait_bytes(stage.at[pl.ds(0, FAR_IN)], far_send)
        wait_bytes(stage.at[pl.ds(0, (SIDE - 1) * blocks)], share_send)
        wait_bytes(rs_buf.at[pl.ds(0, LINE - 1)], ar_send.at[0])
        wait_bytes(plane_buf.at[pl.ds(0, PLANE - 1)], ar_send.at[1])
        wait_bytes(gathered.at[pl.ds(0, LINE - 1)], ar_send.at[2])

        total_rows = float(blocks * tile * NG * NZ)
        inverse_factor(gathered[...].reshape(width, width) / total_rows, work, inverse)

        def make_vectors(r, carry):
            rows = pl.ds(pl.multiple_of(r * tile, tile), tile)
            block = lax.dot_general(
                product[rows, :], inverse[...], (((1,), (1,)), ((), ())),
                precision=lax.Precision.HIGHEST, preferred_element_type=jnp.float32,
            )
            if it == ITERS - 1:
                vectors_out[rows, :] = block
            else:
                per_step[it + 1][0][r] = block.astype(start.dtype)
            return carry

        lax.fori_loop(0, blocks, make_vectors, 0)


def iterate(near_cols, far_groups, need, start, tiles_near, tiles_far):
    blocks, tile, width = start.shape
    rows = width // LINE
    step_buffers = (
        [pltpu.VMEM((blocks, tile, width), start.dtype)] * (NZ + SIDE - 1)
        + [
            pltpu.VMEM((NG, tile, width), start.dtype),
            pltpu.VMEM((LINE, rows, width), jnp.float32),
            pltpu.VMEM((rows, width), jnp.float32),
            pltpu.VMEM((PLANE, rows, width), jnp.float32),
            pltpu.VMEM((rows, width), jnp.float32),
            pltpu.VMEM((LINE, rows, width), jnp.float32),
        ]
    )
    assert len(step_buffers) == STEP_BUFFERS
    return pl.pallas_call(
        iteration_kernel,
        out_shape=jax.ShapeDtypeStruct((blocks * tile, width), jnp.float32),
        in_specs=[pl.BlockSpec(memory_space=pltpu.SMEM)] * 3
        + [pl.BlockSpec(memory_space=pltpu.VMEM)]
        + [pl.BlockSpec(memory_space=pltpu.HBM)] * 2,
        out_specs=pl.BlockSpec(memory_space=pltpu.VMEM),
        scratch_shapes=[
            pltpu.VMEM(tiles_near.shape, tiles_near.dtype),
            pltpu.VMEM(tiles_far.shape, tiles_far.dtype),
            pltpu.VMEM((NG, tile, width), start.dtype),
            pltpu.VMEM((NC, SIDE, SIDE, 8, 128), jnp.float32),
            pltpu.VMEM((NC * SIDE, SIDE, 8, 128), jnp.float32),
            pltpu.VMEM((blocks * tile, width), jnp.float32),
            pltpu.VMEM((LINE, rows, width), jnp.float32),
            pltpu.VMEM((width, 2 * width), jnp.float32),
            pltpu.VMEM((width, width), jnp.float32),
        ]
        + step_buffers * ITERS
        + [
            pltpu.SemaphoreType.DMA((2,)),
            pltpu.SemaphoreType.DMA((2,)),
            pltpu.SemaphoreType.DMA((ITERS, 2, NZ // 2, 2)),
            pltpu.SemaphoreType.DMA,
            pltpu.SemaphoreType.DMA,
            pltpu.SemaphoreType.DMA,
            pltpu.SemaphoreType.DMA((ITERS, SIDE - 1)),
            pltpu.SemaphoreType.DMA,
            pltpu.SemaphoreType.DMA((ITERS,)),
            pltpu.SemaphoreType.DMA((3,)),
            pltpu.SemaphoreType.DMA((ITERS, 3)),
        ],
        compiler_params=pltpu.CompilerParams(
            collective_id=0, has_side_effects=True, vmem_limit_bytes=60 << 20
        ),
        name="iterate",
    )(near_cols, far_groups, need, start, tiles_near, tiles_far)


def per_device(tiles_near, near_cols, tiles_far, far_groups, need_blocks, start_vectors):
    tile_size = tiles_near.shape[1]
    rows, vec_width = start_vectors.shape
    start = start_vectors.reshape(rows // tile_size, tile_size, vec_width)
    return iterate(near_cols, far_groups, need_blocks, start, tiles_near, tiles_far)


def solution(mesh):
    in_specs = (
        P(("grp", "blk"), None, None),
        P(("grp", "blk"), None),
        P(("grp", "blk"), None, None),
        P(("grp", "blk"), None),
        P(("grp", "blk"), None),
        P(("grp", "blk"), None),
    )
    out_specs = P(("grp", "blk"), None)
    return jax.shard_map(
        per_device, mesh=mesh, in_specs=in_specs, out_specs=out_specs, check_vma=False
    )
```

```python
import functools

import jax
import jax.numpy as jnp
from jax import lax
from jax.experimental import pallas as pl
from jax.experimental.pallas import tpu as pltpu
from jax.sharding import PartitionSpec as P

ITERS = 2
MESH = pl.DeviceIdType.MESH
NX, NY, NC, NZ = 4, 4, 2, 8
NG = NX * NY * NC
LINE = NC * NZ
PLANE = NX * NY
PANEL = 16
SIDE = NX
FAR_IN = SIDE * (NC * SIDE - 1)


def wait_bytes(ref, sem):
    pltpu.make_async_copy(ref, ref, sem).wait()


def split(value):
    high = value.astype(jnp.bfloat16)
    rest = value - high.astype(jnp.float32)
    middle = rest.astype(jnp.bfloat16)
    return high, middle, (rest - middle.astype(jnp.float32)).astype(jnp.bfloat16)


def start_factor(gram, work):
    n = gram.shape[0]
    row_id = lax.broadcasted_iota(jnp.int32, (n, n), 0)
    col_id = lax.broadcasted_iota(jnp.int32, (n, n), 1)
    work[:, :n] = gram
    work[:, n:] = (row_id == col_id).astype(jnp.float32)


def factor_panels(work, out, first, last):
    n = out.shape[0]
    sub = lax.broadcasted_iota(jnp.int32, (8, 2 * n), 0)

    def wide(value):
        return jnp.concatenate([value] * 2, 1)

    def panel(p, carry):
        start = pl.multiple_of(p * PANEL, PANEL)
        rows = pl.ds(start, PANEL)
        top = work[rows, :]
        diag = pltpu.roll(top[:, :n], lax.rem(n - start, n), 1)
        a, low, scale, solved = {}, {}, [], []
        for j in range(PANEL):
            for i in range(j, PANEL):
                a[i, j] = jnp.broadcast_to(diag[i : i + 1, j : j + 1], (8, n))
        for j in range(PANEL):
            scale.append(lax.rsqrt(a[j, j]))
            for i in range(j + 1, PANEL):
                low[i, j] = a[i, j] * scale[j]
            for k in range(j + 1, PANEL):
                for i in range(k, PANEL):
                    a[i, k] = a[i, k] - low[i, j] * low[k, j]
        for j in range(PANEL):
            row = jnp.broadcast_to(top[j : j + 1, :], (8, 2 * n))
            for k in range(j):
                row = row - wide(low[j, k]) * solved[k]
            solved.append(row * wide(scale[j]))
        pieces = []
        for b in range(0, PANEL, 8):
            piece = solved[b]
            for j in range(1, 8):
                piece = jnp.where(sub == j, solved[b + j], piece)
            pieces.append(piece)
        block = jnp.concatenate(pieces, 0)
        out[rows, :] = block[:, n:]
        high, middle, small = split(block)
        left = jnp.concatenate([v[:, :n] for v in (high, high, middle, high, small, middle)], 0)
        right = jnp.concatenate([high, middle, high, small, high, middle], 0)
        work[...] = work[...] - lax.dot_general(
            left, right, (((0,), (0,)), ((), ())), preferred_element_type=jnp.float32
        )
        return carry

    lax.fori_loop(first, last, panel, 0)


def iteration_kernel(names, *refs):
    ref = dict(zip(names, refs))
    near_cols, far_groups, need, start = ref["near_cols"], ref["far_groups"], ref["need"], ref["start"]
    a_near, a_far, request, wanted = ref["a_near"], ref["a_far"], ref["request"], ref["wanted"]
    product, early, work, inverse = ref["product"], ref["early"], ref["work"], ref["inverse"]
    gram = ref["gram"]

    g = lax.axis_index("grp")
    z = lax.axis_index("blk")
    core = lax.rem(g, NC)
    xy = g // NC
    x, y = xy // NY, lax.rem(xy, NY)
    blocks, tile, width = start.shape
    q = z * NC + core
    low_half = lax.broadcasted_iota(jnp.int32, (tile, width), 1) < width // 2
    half_id = lax.broadcasted_iota(jnp.int32, (tile, width), 1) // (width // 2)

    load_near = pltpu.make_async_copy(ref["tiles_near"], a_near, ref["tile_sem"].at[0])
    load_far = pltpu.make_async_copy(ref["tiles_far"], a_far, ref["tile_sem"].at[1])
    load_near.start()
    load_far.start()

    def group_at(first, second, which):
        px = first + which * (second - first)
        py = second + which * (first - second)
        return px * NY + py

    axis_a = x + core * (y - x)
    axis_b = y + core * (x - y)

    def same_core(first, second):
        return group_at(first, second, core) * NC + core

    def group_peer(k):
        dc, dy, dx = lax.rem(k, NC), lax.rem(k // NC, NY), k // (NC * NY)
        px, py, pc = lax.rem(x + dx, NX), lax.rem(y + dy, NY), lax.rem(core + dc, NC)
        return (px * NY + py) * NC + pc

    def line_peer(k):
        pz, pc = lax.rem(z + k // NC, NZ), lax.rem(core + lax.rem(k, NC), NC)
        return xy * NC + pc, pz

    def plane_peer(k):
        px, py = lax.rem(x + k // NY, NX), lax.rem(y + lax.rem(k, NY), NY)
        return (px * NY + py) * NC + core

    def loop(first, last, body):
        def step(k, carry):
            body(k)
            return carry

        lax.fori_loop(first, last, step, 0)

    def block_rows(r):
        return pl.ds(pl.multiple_of(r * tile, tile), tile)

    barrier = pltpu.get_barrier_semaphore()

    def greet_group(k):
        pl.semaphore_signal(barrier, inc=1, device_id=(group_peer(k), z), device_id_type=MESH)

    def greet_line(k):
        pl.semaphore_signal(barrier, inc=1, device_id=line_peer(k), device_id_type=MESH)

    loop(1, NG, greet_group)
    loop(NC, LINE, greet_line)

    def fill_request(k):
        t, b, a = k // (SIDE * SIDE), lax.rem(k // SIDE, SIDE), lax.rem(k, SIDE)
        source = group_at(a, b, t) * NC + t
        value = jnp.full(request.shape[3:], need[0, source], jnp.int32).astype(jnp.float32)
        request[t, b, a] = value

    loop(0, NG, fill_request)
    wanted[axis_b * NC + core] = request[core, axis_b]
    ref["own0"][...] = start[...]
    pl.semaphore_wait(barrier, NG - 1 + LINE - NC)

    right, left = lax.rem(z + 1, NZ), lax.rem(z + NZ - 1, NZ)
    last = NZ // 2 - 1
    seven = wanted.at[pl.ds(0, NC * SIDE - 1)]

    def send_request(k):
        t = lax.rem(core + k // SIDE, NC)
        mine_a, mine_b = x + t * (y - x), y + t * (x - y)
        b = lax.rem(mine_b + lax.rem(k, SIDE), SIDE)
        relay = group_at(mine_a, b, t) * NC + t
        pltpu.make_async_remote_copy(
            src_ref=request.at[t, b], dst_ref=wanted.at[mine_b * NC + core],
            send_sem=ref["req_sem"].at[0], recv_sem=ref["req_sem"].at[1],
            device_id=(relay, z), device_id_type=MESH,
        ).start()

    near_row = a_near.shape[0] // blocks
    per_source = near_row // NZ
    far_row = a_far.shape[0] // blocks

    def parts(direction, step):
        if step < last:
            return (0, 1) if direction == 0 else (1, 0)
        return (direction,)

    class Round:
        def __init__(self, index):
            self.index, self.packed = index, index == 2
            self.own = ref["own%d" % index]
            self.away = [ref["away%d_%d" % (index, i)] for i in range(NZ - 1)]
            self.shared = ref["rows2"] if self.packed else self.own
            self.relay = [ref["relay%d_%d" % (index, i)] for i in range(SIDE - 1)]
            self.far = ref["far%d" % index]
            self.stage = ref["stage2" if self.packed else "stage"]
            self.half = self.own.shape[0] // 2

        def slot(self, direction, step):
            return self.away[2 * last] if step == last else self.away[2 * step + direction]

        def ring(self, direction, step, part):
            rows = pl.ds(part * self.half, self.half)
            src = self.own if step == 0 else self.slot(direction, step - 1)
            return pltpu.make_async_remote_copy(
                src_ref=src.at[rows], dst_ref=self.slot(direction, step).at[rows],
                send_sem=ref["ring_send"].at[self.index, direction],
                recv_sem=ref["ring_recv"].at[self.index, direction, step, part],
                device_id=(g, left if direction else right), device_id_type=MESH,
            )

        def share(self, k):
            return pltpu.make_async_remote_copy(
                src_ref=self.shared, dst_ref=self.relay[SIDE - k - 1],
                send_sem=ref["share_send"].at[self.index],
                recv_sem=ref["share_recv"].at[self.index, SIDE - k - 1],
                device_id=(same_core(lax.rem(axis_a + k, SIDE), axis_b), z), device_id_type=MESH,
            )

        def begin(self):
            for i in range(2):
                for direction in (0, 1):
                    self.ring(direction, 0, parts(direction, 0)[i]).start()
            for k in (1, 3, 2):
                self.share(k).start()

        def choose(self, shard, ask):
            choice = ask[None]
            picked = shard[0].astype(jnp.float32).reshape(-1, 8, 128)
            for b in range(1, blocks):
                other = shard[b].astype(jnp.float32).reshape(-1, 8, 128)
                picked = jnp.where(choice == float(b), other, picked)
            return picked.reshape(self.far.shape[1:]).astype(start.dtype)

        def pass_on(self, away_by):
            if away_by:
                self.share(SIDE - away_by).wait_recv()
            shard = self.relay[away_by - 1] if away_by else self.shared
            a = lax.rem(axis_a + away_by, SIDE)
            source = same_core(a, axis_b)

            def send_one(m):
                b, c = lax.rem(axis_b + m // NC, SIDE), lax.rem(core + lax.rem(m, NC), NC)
                spot = away_by * (NC * SIDE - 1) + m - 1
                self.stage[spot] = self.choose(shard, wanted[b * NC + c, a])
                pltpu.make_async_remote_copy(
                    src_ref=self.stage.at[spot], dst_ref=self.far.at[source],
                    send_sem=ref["far_send"].at[self.index],
                    recv_sem=ref["far_recv"].at[self.index],
                    device_id=(group_at(axis_a, b, core) * NC + c, z), device_id_type=MESH,
                ).start()

            loop(1, NC * SIDE, send_one)
            self.far[source] = self.choose(shard, wanted[axis_b * NC + core, a])

        def forward(self, step, i):
            for direction in (0, 1):
                if i < len(parts(direction, step)):
                    here = parts(direction, step)[i]
                    self.ring(direction, step, here).wait_recv()
                    if step < last and here in parts(direction, step + 1):
                        self.ring(direction, step + 1, here).start()

        def near(self, shard, source, total, first):
            def one_row(r):
                acc = None if first else total[block_rows(r), :]
                for n in range(per_source):
                    t = r * near_row + source * per_source + n
                    col = near_cols[0, t]
                    if self.packed:
                        pair = shard[lax.shift_right_logical(col, 1)]
                        term = jnp.dot(a_near[t], pair, preferred_element_type=jnp.float32)
                        term = jnp.where(half_id == jnp.bitwise_and(col, 1), term, 0.0)
                    else:
                        term = jnp.dot(
                            a_near[t], shard[col], preferred_element_type=jnp.float32
                        )
                    acc = term if acc is None else acc + term
                total[block_rows(r), :] = acc

            loop(0, blocks, one_row)

        def near_own(self, total):
            self.near(self.own, z, total, True)

        def near_step(self, step, total):
            self.near(self.slot(0, step), lax.rem(z + NZ - 1 - step, NZ), total, False)
            if step < last:
                self.near(self.slot(1, step), lax.rem(z + 1 + step, NZ), total, False)

        def far_all(self, total):
            wait_bytes(self.far.at[pl.ds(0, FAR_IN)], ref["far_recv"].at[self.index])
            middle = tile // 2

            def one_row(r):
                acc = total[block_rows(r), :]
                for j in range(far_row):
                    t = r * far_row + j
                    block = self.far[far_groups[0, t]]
                    if self.packed:
                        upper = jnp.dot(
                            a_far[t, :, :middle], block, preferred_element_type=jnp.float32
                        )
                        lower = jnp.dot(
                            a_far[t, :, middle:], block, preferred_element_type=jnp.float32
                        )
                        acc += jnp.where(low_half, upper, lower)
                    else:
                        acc += jnp.dot(a_far[t], block, preferred_element_type=jnp.float32)
                total[block_rows(r), :] = acc

            loop(0, blocks, one_row)

        def finish(self):
            sent = (last + 1) * blocks - blocks // 2
            for direction in (0, 1):
                wait_bytes(
                    self.far.at[pl.ds(0, sent)], ref["ring_send"].at[self.index, direction]
                )
            wait_bytes(self.stage.at[pl.ds(0, FAR_IN)], ref["far_send"].at[self.index])
            wait_bytes(
                self.stage.at[pl.ds(0, (SIDE - 1) * blocks)], ref["share_send"].at[self.index]
            )

    class GramSum:
        def __init__(self, it):
            self.it = it
            self.bufs = [ref["%s%d" % (n, it)] for n in ("rs", "part", "plane", "total", "gathered")]

        def send(self, phase, src, dst, device):
            pltpu.make_async_remote_copy(
                src_ref=src, dst_ref=dst,
                send_sem=ref["ar_send"].at[self.it, phase],
                recv_sem=ref["ar_recv"].at[self.it, phase],
                device_id=device, device_id_type=MESH,
            ).start()

        def scatter(self):
            rs = self.bufs[0]
            flat = product[...]
            gram[...] = lax.dot_general(
                flat, flat, (((0,), (0,)), ((), ())),
                precision=lax.Precision.HIGHEST, preferred_element_type=jnp.float32,
            ).reshape(gram.shape)

            def one(k):
                pg, pz = line_peer(k)
                self.send(0, gram.at[pz * NC + lax.rem(pg, NC)], rs.at[q], (pg, pz))

            loop(1, LINE, one)
            rs[q] = gram[q]

        def spread(self):
            rs, part, plane = self.bufs[:3]
            wait_bytes(rs.at[pl.ds(0, LINE - 1)], ref["ar_recv"].at[self.it, 0])
            part[...] = jnp.sum(rs[...], axis=0)
            plane[xy] = part[...]
            loop(1, PLANE, lambda k: self.send(1, part, plane.at[xy], (plane_peer(k), z)))

        def collect(self):
            plane, total, gathered = self.bufs[2:]
            wait_bytes(plane.at[pl.ds(0, PLANE - 1)], ref["ar_recv"].at[self.it, 1])
            total[...] = jnp.sum(plane[...], axis=0)
            gathered[q] = total[...]
            loop(1, LINE, lambda k: self.send(2, total, gathered.at[q], line_peer(k)))

        def result(self):
            gathered = self.bufs[4]
            wait_bytes(gathered.at[pl.ds(0, LINE - 1)], ref["ar_recv"].at[self.it, 2])
            return gathered[...].reshape(width, width) / float(blocks * tile * NG * NZ)

        def finish(self):
            rs, _, plane, _, gathered = self.bufs
            wait_bytes(rs.at[pl.ds(0, LINE - 1)], ref["ar_send"].at[self.it, 0])
            wait_bytes(plane.at[pl.ds(0, PLANE - 1)], ref["ar_send"].at[self.it, 1])
            wait_bytes(gathered.at[pl.ds(0, LINE - 1)], ref["ar_send"].at[self.it, 2])

    panels = width // PANEL
    to_vectors = (((1,), (1,)), ((), ()))

    def times_inverse(value, factor):
        return lax.dot_general(
            value, factor, to_vectors,
            precision=lax.Precision.HIGHEST, preferred_element_type=jnp.float32,
        )

    first = Round(0)
    first.begin()
    loop(1, 2 * SIDE, send_request)
    wait_bytes(seven, ref["req_sem"].at[1])
    first.pass_on(0)
    load_near.wait()
    load_far.wait()
    first.forward(0, 0)
    first.forward(0, 1)
    first.near_own(product)
    for k in (1, 3, 2):
        first.pass_on(k)
    for step in range(last + 1):
        if step:
            first.forward(step, 0)
            first.forward(step, 1)
        first.near_step(step, product)
    first.far_all(product)
    first.finish()
    wait_bytes(seven, ref["req_sem"].at[0])

    ahead, late = Round(1), Round(2)

    def make_early(r):
        rows = product[block_rows(r), :]
        both = jnp.where(low_half, rows, pltpu.roll(rows, width // 2, 1))
        high = both.astype(start.dtype).astype(jnp.float32)
        ahead.own[r] = jnp.where(low_half, high, both - high).astype(start.dtype)

    loop(0, blocks, make_early)
    ahead.begin()
    sums = GramSum(0)
    sums.scatter()
    ahead.pass_on(0)
    sums.spread()
    ahead.forward(0, 0)
    sums.collect()
    ahead.forward(0, 1)
    ahead.pass_on(1)
    ahead.pass_on(3)
    ahead.pass_on(2)
    start_factor(sums.result(), work)
    ahead.forward(1, 0)
    factor_panels(work, inverse, 0, panels // 2)
    ahead.forward(1, 1)
    factor_panels(work, inverse, panels // 2, panels)

    upper = inverse[width // 2 :, :]
    twice = jnp.concatenate([upper, upper], 0)

    def make_late(i):
        even = times_inverse(product[block_rows(2 * i), :], twice)
        odd = times_inverse(product[block_rows(2 * i + 1), :], twice)
        late.own[i] = jnp.where(low_half, even, odd).astype(start.dtype)
        for j, v in enumerate((even, odd)):
            packed = jnp.where(low_half[: tile // 2], v[: tile // 2], v[tile // 2 :])
            late.shared[2 * i + j] = packed.astype(start.dtype)

    loop(0, blocks // 2, make_late)

    late.begin()
    ahead.forward(2, 0)
    late.pass_on(0)
    ahead.near_own(early)
    ahead.forward(2, 1)
    ahead.near_step(0, early)
    late.forward(0, 0)
    late.forward(0, 1)
    late.pass_on(1)
    late.pass_on(3)
    late.pass_on(2)
    ahead.near_step(1, early)
    ahead.forward(3, 0)
    late.forward(1, 0)
    ahead.near_step(2, early)
    late.forward(1, 1)
    ahead.near_step(3, early)
    ahead.far_all(early)
    late.forward(2, 0)
    late.near_own(product)
    late.forward(2, 1)
    late.near_step(0, product)
    late.near_step(1, product)

    def finish_early(r):
        value = early[block_rows(r), :]
        early[block_rows(r), :] = times_inverse(
            value + pltpu.roll(value, width // 2, 1), inverse[...]
        )

    loop(0, blocks, finish_early)
    late.near_step(2, product)
    late.forward(3, 0)
    late.near_step(3, product)
    late.far_all(product)

    def join(r):
        value = product[block_rows(r), :]
        value = value + pltpu.roll(value, width // 2, 1)
        product[block_rows(r), :] = jnp.where(low_half, early[block_rows(r), :], value)

    loop(0, blocks, join)
    sums.finish()
    sums = GramSum(1)
    sums.scatter()
    ahead.finish()
    late.finish()
    sums.spread()
    sums.collect()
    start_factor(sums.result(), work)
    factor_panels(work, inverse, 0, panels)

    def make_vectors(r):
        ref["vectors"][block_rows(r), :] = times_inverse(product[block_rows(r), :], inverse[...])

    loop(0, blocks, make_vectors)
    sums.finish()


def iterate(near_cols, far_groups, need, start, tiles_near, tiles_far):
    blocks, tile, width = start.shape
    rows = width // LINE
    f32, dtype = jnp.float32, start.dtype
    scratch = {
        "a_near": pltpu.VMEM(tiles_near.shape, dtype),
        "a_far": pltpu.VMEM(tiles_far.shape, dtype),
        "request": pltpu.VMEM((NC, SIDE, SIDE, 8, 128), f32),
        "wanted": pltpu.VMEM((NC * SIDE, SIDE, 8, 128), f32),
        "product": pltpu.VMEM((blocks * tile, width), f32),
        "early": pltpu.VMEM((blocks * tile, width), f32),
        "gram": pltpu.VMEM((LINE, rows, width), f32),
        "work": pltpu.VMEM((width, 2 * width), f32),
        "inverse": pltpu.VMEM((width, width), f32),
        "stage": pltpu.VMEM((NG, tile, width), dtype),
        "stage2": pltpu.VMEM((NG, tile // 2, width), dtype),
        "rows2": pltpu.VMEM((blocks, tile // 2, width), dtype),
    }
    for index in range(3):
        shard = (blocks // 2 if index == 2 else blocks, tile, width)
        height = tile // 2 if index == 2 else tile
        scratch["own%d" % index] = pltpu.VMEM(shard, dtype)
        for i in range(NZ - 1):
            scratch["away%d_%d" % (index, i)] = pltpu.VMEM(shard, dtype)
        for i in range(SIDE - 1):
            scratch["relay%d_%d" % (index, i)] = pltpu.VMEM((blocks, height, width), dtype)
        scratch["far%d" % index] = pltpu.VMEM((NG, height, width), dtype)
    for it in range(ITERS):
        scratch["rs%d" % it] = pltpu.VMEM((LINE, rows, width), f32)
        scratch["part%d" % it] = pltpu.VMEM((rows, width), f32)
        scratch["plane%d" % it] = pltpu.VMEM((PLANE, rows, width), f32)
        scratch["total%d" % it] = pltpu.VMEM((rows, width), f32)
        scratch["gathered%d" % it] = pltpu.VMEM((LINE, rows, width), f32)
    dma = pltpu.SemaphoreType.DMA
    scratch["tile_sem"] = dma((2,))
    scratch["req_sem"] = dma((2,))
    scratch["ring_send"] = dma((3, 2))
    scratch["ring_recv"] = dma((3, 2, NZ // 2, 2))
    scratch["share_send"] = dma((3,))
    scratch["share_recv"] = dma((3, SIDE - 1))
    scratch["far_send"] = dma((3,))
    scratch["far_recv"] = dma((3,))
    scratch["ar_send"] = dma((ITERS, 3))
    scratch["ar_recv"] = dma((ITERS, 3))
    operands = ("near_cols", "far_groups", "need", "start", "tiles_near", "tiles_far")
    names = operands + ("vectors",) + tuple(scratch)
    return pl.pallas_call(
        functools.partial(iteration_kernel, names),
        out_shape=jax.ShapeDtypeStruct((blocks * tile, width), jnp.float32),
        in_specs=[pl.BlockSpec(memory_space=pltpu.SMEM)] * 3
        + [pl.BlockSpec(memory_space=pltpu.VMEM)]
        + [pl.BlockSpec(memory_space=pltpu.HBM)] * 2,
        out_specs=pl.BlockSpec(memory_space=pltpu.VMEM),
        scratch_shapes=list(scratch.values()),
        compiler_params=pltpu.CompilerParams(
            collective_id=0, has_side_effects=True, vmem_limit_bytes=60 << 20
        ),
        name="iterate",
    )(near_cols, far_groups, need, start, tiles_near, tiles_far)


def per_device(tiles_near, near_cols, tiles_far, far_groups, need_blocks, start_vectors):
    tile_size = tiles_near.shape[1]
    rows, vec_width = start_vectors.shape
    start = start_vectors.reshape(rows // tile_size, tile_size, vec_width)
    return iterate(near_cols, far_groups, need_blocks, start, tiles_near, tiles_far)


def solution(mesh):
    in_specs = (
        P(("grp", "blk"), None, None),
        P(("grp", "blk"), None),
        P(("grp", "blk"), None, None),
        P(("grp", "blk"), None),
        P(("grp", "blk"), None),
        P(("grp", "blk"), None),
    )
    out_specs = P(("grp", "blk"), None)
    return jax.shard_map(
        per_device, mesh=mesh, in_specs=in_specs, out_specs=out_specs, check_vma=False
    )
```

```python
import jax
import jax.numpy as jnp
from jax import lax
from jax.experimental import pallas as pl
from jax.experimental.pallas import tpu as pltpu
from jax.sharding import PartitionSpec as P

ITERS = 2
MESH = pl.DeviceIdType.MESH
NX, NY, NC, NZ = 4, 4, 2, 8
NG = NX * NY * NC
LINE = NC * NZ
PLANE = NX * NY
PANEL = 16
SIDE = NX
STEP_BUFFERS = NZ + SIDE - 1 + 6
FAR_IN = SIDE * (NC * SIDE - 1)


def wait_bytes(ref, sem):
    pltpu.make_async_copy(ref, ref, sem).wait()


def split(value):
    high = value.astype(jnp.bfloat16)
    rest = value - high.astype(jnp.float32)
    middle = rest.astype(jnp.bfloat16)
    return high, middle, (rest - middle.astype(jnp.float32)).astype(jnp.bfloat16)


def inverse_factor(gram, work, out):
    n = gram.shape[0]
    row_id = lax.broadcasted_iota(jnp.int32, (n, n), 0)
    col_id = lax.broadcasted_iota(jnp.int32, (n, n), 1)
    work[:, :n] = gram
    work[:, n:] = (row_id == col_id).astype(jnp.float32)
    sub = lax.broadcasted_iota(jnp.int32, (8, 2 * n), 0)

    def wide(value):
        return jnp.concatenate([value] * 2, 1)

    def panel(p, carry):
        start = pl.multiple_of(p * PANEL, PANEL)
        rows = pl.ds(start, PANEL)
        top = work[rows, :]
        diag = pltpu.roll(top[:, :n], lax.rem(n - start, n), 1)
        a, low, scale, solved = {}, {}, [], []
        for j in range(PANEL):
            for i in range(j, PANEL):
                a[i, j] = jnp.broadcast_to(diag[i : i + 1, j : j + 1], (8, n))
        for j in range(PANEL):
            scale.append(lax.rsqrt(a[j, j]))
            for i in range(j + 1, PANEL):
                low[i, j] = a[i, j] * scale[j]
            for k in range(j + 1, PANEL):
                for i in range(k, PANEL):
                    a[i, k] = a[i, k] - low[i, j] * low[k, j]
        for j in range(PANEL):
            row = jnp.broadcast_to(top[j : j + 1, :], (8, 2 * n))
            for k in range(j):
                row = row - wide(low[j, k]) * solved[k]
            solved.append(row * wide(scale[j]))
        pieces = []
        for b in range(0, PANEL, 8):
            piece = solved[b]
            for j in range(1, 8):
                piece = jnp.where(sub == j, solved[b + j], piece)
            pieces.append(piece)
        block = jnp.concatenate(pieces, 0)
        out[rows, :] = block[:, n:]
        high, middle, small = split(block)
        left = jnp.concatenate([v[:, :n] for v in (high, high, middle, high, small, middle)], 0)
        right = jnp.concatenate([high, middle, high, small, high, middle], 0)
        work[...] = work[...] - lax.dot_general(
            left, right, (((0,), (0,)), ((), ())), preferred_element_type=jnp.float32
        )
        return carry

    lax.fori_loop(0, n // PANEL, panel, 0)


def iteration_kernel(*refs):
    (near_cols, far_groups, need, start, tiles_near, tiles_far, vectors_out,
     a_near, a_far, stage, request, wanted, product, gram, work, inverse) = refs[:16]
    refs = refs[16:]
    per_step = [refs[i * STEP_BUFFERS : (i + 1) * STEP_BUFFERS] for i in range(ITERS)]
    (tile_sem, ring_send, ring_recv, req_send, req_recv, share_send, share_recv, far_send, far_recv,
     ar_send, ar_recv) = refs[ITERS * STEP_BUFFERS :]

    g = lax.axis_index("grp")
    z = lax.axis_index("blk")
    core = lax.rem(g, NC)
    xy = g // NC
    x, y = xy // NY, lax.rem(xy, NY)
    blocks, tile, width = start.shape
    half = blocks // 2
    rows_each = width // LINE
    q = z * NC + core

    load_near = pltpu.make_async_copy(tiles_near, a_near, tile_sem.at[0])
    load_far = pltpu.make_async_copy(tiles_far, a_far, tile_sem.at[1])
    load_near.start()
    load_far.start()

    def group_at(first, second, which):
        px = first + which * (second - first)
        py = second + which * (first - second)
        return px * NY + py

    axis_a = x + core * (y - x)
    axis_b = y + core * (x - y)

    def same_core(first, second):
        return group_at(first, second, core) * NC + core

    def line_peer(k):
        pz, pc = lax.rem(z + k // NC, NZ), lax.rem(core + (k % NC), NC)
        return xy * NC + pc, pz

    def plane_peer(k):
        px, py = lax.rem(x + k // NY, NX), lax.rem(y + (k % NY), NY)
        return (px * NY + py) * NC + core

    line_order = sorted(range(1, LINE), key=lambda k: -min(k // NC, NZ - k // NC))
    plane_order = sorted(
        range(1, PLANE), key=lambda k: -min(k // NY, NX - k // NY) - min(k % NY, NY - k % NY)
    )
    barrier = pltpu.get_barrier_semaphore()

    def greet(group, position):
        pl.semaphore_signal(barrier, inc=1, device_id=(group, position), device_id_type=MESH)

    def greet_line(k, carry):
        greet(*line_peer(k))
        return carry

    def greet_plane(k, carry):
        greet(plane_peer(k), z)
        return carry

    def greet_cross(k, carry):
        greet(group_at(axis_a, lax.rem(axis_b + k, SIDE), core) * NC + 1 - core, z)
        greet(group_at(lax.rem(axis_a + k, SIDE), axis_b, core) * NC + 1 - core, z)
        return carry

    lax.fori_loop(1, LINE, greet_line, 0)
    lax.fori_loop(1, PLANE, greet_plane, 0)
    lax.fori_loop(1, SIDE, greet_cross, 0)

    def fill_request(k, carry):
        t, b, a = k // (SIDE * SIDE), lax.rem(k // SIDE, SIDE), lax.rem(k, SIDE)
        source = group_at(a, b, t) * NC + t
        value = jnp.full(request.shape[3:], need[0, source], jnp.int32).astype(jnp.float32)
        request[t, b, a] = value
        return carry

    lax.fori_loop(0, NG, fill_request, 0)
    wanted[axis_b * NC + core] = request[core, axis_b]
    per_step[0][0][...] = start[...]
    pl.semaphore_wait(barrier, LINE - 1 + PLANE - 1 + 2 * (SIDE - 1))

    right, left = lax.rem(z + 1, NZ), lax.rem(z + NZ - 1, NZ)
    last = NZ // 2 - 1

    def parts(direction, step):
        if step < last:
            return (0, 1) if direction == 0 else (1, 0)
        return (direction,)

    def send_request(k, carry):
        t = lax.rem(core + k // SIDE, NC)
        mine_a, mine_b = x + t * (y - x), y + t * (x - y)
        b = lax.rem(mine_b + lax.rem(k, SIDE), SIDE)
        relay = group_at(mine_a, b, t) * NC + t
        pltpu.make_async_remote_copy(
            src_ref=request.at[t, b], dst_ref=wanted.at[mine_b * NC + core],
            send_sem=req_send, recv_sem=req_recv,
            device_id=(relay, z), device_id_type=MESH,
        ).start()
        return carry

    near_row = a_near.shape[0] // blocks
    per_source = near_row // NZ
    far_row = a_far.shape[0] // blocks

    for it in range(ITERS):
        own, away = per_step[it][0], per_step[it][1 : NZ]
        relay_buf = per_step[it][NZ : NZ + SIDE - 1]
        far_buf, rs_buf, part, plane_buf, total, gathered = per_step[it][NZ + SIDE - 1 :]

        def slot(direction, step):
            return away[2 * last] if step == last else away[2 * step + direction]

        def ring(direction, step, part_id):
            rows = pl.ds(part_id * half, half)
            src = own if step == 0 else slot(direction, step - 1)
            return pltpu.make_async_remote_copy(
                src_ref=src.at[rows],
                dst_ref=slot(direction, step).at[rows],
                send_sem=ring_send.at[direction],
                recv_sem=ring_recv.at[it, direction, step, part_id],
                device_id=(g, left if direction else right),
                device_id_type=MESH,
            )

        for i in range(2):
            for direction in (0, 1):
                ring(direction, 0, parts(direction, 0)[i]).start()

        if it == 0:
            lax.fori_loop(1, 2 * SIDE, send_request, 0)

        def share(k):
            return pltpu.make_async_remote_copy(
                src_ref=own, dst_ref=relay_buf[SIDE - k - 1],
                send_sem=share_send, recv_sem=share_recv.at[it, SIDE - k - 1],
                device_id=(same_core(lax.rem(axis_a + k, SIDE), axis_b), z), device_id_type=MESH,
            )

        for k in (1, 3, 2):
            share(k).start()
        if it == 0:
            wait_bytes(wanted.at[pl.ds(0, NC * SIDE - 1)], req_recv)

        def choose(shard, ask):
            choice = ask[None]
            picked = shard[0].astype(jnp.float32).reshape(-1, 8, 128)
            for b in range(1, blocks):
                other = shard[b].astype(jnp.float32).reshape(-1, 8, 128)
                picked = jnp.where(choice == float(b), other, picked)
            return picked.reshape(tile, width).astype(start.dtype)

        def pass_on(away_by):
            shard = own if away_by == 0 else relay_buf[away_by - 1]
            a = lax.rem(axis_a + away_by, SIDE)
            source = same_core(a, axis_b)

            def send_one(m, carry):
                b, c = lax.rem(axis_b + m // NC, SIDE), lax.rem(core + lax.rem(m, NC), NC)
                spot = away_by * (NC * SIDE - 1) + m - 1
                stage[spot] = choose(shard, wanted[b * NC + c, a])
                pltpu.make_async_remote_copy(
                    src_ref=stage.at[spot], dst_ref=far_buf.at[source],
                    send_sem=far_send, recv_sem=far_recv.at[it],
                    device_id=(group_at(axis_a, b, core) * NC + c, z), device_id_type=MESH,
                ).start()
                return carry

            lax.fori_loop(1, NC * SIDE, send_one, 0)
            far_buf[source] = choose(shard, wanted[axis_b * NC + core, a])

        pass_on(0)

        def near_part(shard, source, first):
            def one_row(r, carry):
                rows = pl.ds(pl.multiple_of(r * tile, tile), tile)
                acc = None if first else product[rows, :]
                for n in range(per_source):
                    t = r * near_row + source * per_source + n
                    term = jnp.dot(
                        a_near[t], shard[near_cols[0, t]], preferred_element_type=jnp.float32
                    )
                    acc = term if acc is None else acc + term
                product[rows, :] = acc
                return carry

            lax.fori_loop(0, blocks, one_row, 0, unroll=True)

        def far_rows(r, carry):
            rows = pl.ds(pl.multiple_of(r * tile, tile), tile)
            acc = product[rows, :]
            for j in range(far_row):
                t = r * far_row + j
                acc += jnp.dot(
                    a_far[t], far_buf[far_groups[0, t]], preferred_element_type=jnp.float32
                )
            product[rows, :] = acc
            return carry

        def forward(step):
            for i in range(2):
                for direction in (0, 1):
                    if i < len(parts(direction, step)):
                        here = parts(direction, step)[i]
                        ring(direction, step, here).wait_recv()
                        if step < last and here in parts(direction, step + 1):
                            ring(direction, step + 1, here).start()

        if it == 0:
            load_near.wait()
            load_far.wait()
        near_part(own, z, True)
        forward(0)
        for k in (1, 3, 2):
            share(SIDE - k).wait_recv()
            pass_on(k)
        for step in range(last):
            if step:
                forward(step)
            near_part(slot(0, step), lax.rem(z + NZ - 1 - step, NZ), False)
            near_part(slot(1, step), lax.rem(z + 1 + step, NZ), False)
        wait_bytes(far_buf.at[pl.ds(0, FAR_IN)], far_recv.at[it])
        lax.fori_loop(0, blocks, far_rows, 0, unroll=True)
        forward(last)
        near_part(slot(0, last), lax.rem(z + NZ // 2, NZ), False)

        flat = product[...]
        gram[...] = lax.dot_general(
            flat, flat, (((0,), (0,)), ((), ())),
            precision=lax.Precision.HIGHEST, preferred_element_type=jnp.float32,
        ).reshape(gram.shape)

        def scatter(k, carry):
            pg, pz = line_peer(k)
            pltpu.make_async_remote_copy(
                src_ref=gram.at[pz * NC + lax.rem(pg, NC)], dst_ref=rs_buf.at[q],
                send_sem=ar_send.at[0], recv_sem=ar_recv.at[it, 0],
                device_id=(pg, pz), device_id_type=MESH,
            ).start()
            return carry

        for k in line_order:
            scatter(k, 0)
        rs_buf[q] = gram[q]
        wait_bytes(rs_buf.at[pl.ds(0, LINE - 1)], ar_recv.at[it, 0])
        part[...] = jnp.sum(rs_buf[...], axis=0)
        plane_buf[xy] = part[...]

        def spread(k, carry):
            pltpu.make_async_remote_copy(
                src_ref=part, dst_ref=plane_buf.at[xy],
                send_sem=ar_send.at[1], recv_sem=ar_recv.at[it, 1],
                device_id=(plane_peer(k), z), device_id_type=MESH,
            ).start()
            return carry

        for k in plane_order:
            spread(k, 0)
        wait_bytes(plane_buf.at[pl.ds(0, PLANE - 1)], ar_recv.at[it, 1])
        total[...] = jnp.sum(plane_buf[...], axis=0)
        gathered[q] = total[...]

        def collect(k, carry):
            pltpu.make_async_remote_copy(
                src_ref=total, dst_ref=gathered.at[q],
                send_sem=ar_send.at[2], recv_sem=ar_recv.at[it, 2],
                device_id=line_peer(k), device_id_type=MESH,
            ).start()
            return carry

        for k in line_order:
            collect(k, 0)
        wait_bytes(gathered.at[pl.ds(0, LINE - 1)], ar_recv.at[it, 2])

        sent = (last + 1) * blocks - half
        for direction in (0, 1):
            wait_bytes(far_buf.at[pl.ds(0, sent)], ring_send.at[direction])
        if it == 0:
            wait_bytes(wanted.at[pl.ds(0, NC * SIDE - 1)], req_send)
        wait_bytes(stage.at[pl.ds(0, FAR_IN)], far_send)
        wait_bytes(stage.at[pl.ds(0, (SIDE - 1) * blocks)], share_send)
        wait_bytes(rs_buf.at[pl.ds(0, LINE - 1)], ar_send.at[0])
        wait_bytes(plane_buf.at[pl.ds(0, PLANE - 1)], ar_send.at[1])
        wait_bytes(gathered.at[pl.ds(0, LINE - 1)], ar_send.at[2])

        total_rows = float(blocks * tile * NG * NZ)
        inverse_factor(gathered[...].reshape(width, width) / total_rows, work, inverse)

        def make_vectors(r, carry):
            rows = pl.ds(pl.multiple_of(r * tile, tile), tile)
            block = lax.dot_general(
                product[rows, :], inverse[...], (((1,), (1,)), ((), ())),
                precision=lax.Precision.HIGHEST, preferred_element_type=jnp.float32,
            )
            if it == ITERS - 1:
                vectors_out[rows, :] = block
            else:
                per_step[it + 1][0][r] = block.astype(start.dtype)
            return carry

        lax.fori_loop(0, blocks, make_vectors, 0)


def iterate(near_cols, far_groups, need, start, tiles_near, tiles_far):
    blocks, tile, width = start.shape
    rows = width // LINE
    step_buffers = (
        [pltpu.VMEM((blocks, tile, width), start.dtype)] * (NZ + SIDE - 1)
        + [
            pltpu.VMEM((NG, tile, width), start.dtype),
            pltpu.VMEM((LINE, rows, width), jnp.float32),
            pltpu.VMEM((rows, width), jnp.float32),
            pltpu.VMEM((PLANE, rows, width), jnp.float32),
            pltpu.VMEM((rows, width), jnp.float32),
            pltpu.VMEM((LINE, rows, width), jnp.float32),
        ]
    )
    assert len(step_buffers) == STEP_BUFFERS
    return pl.pallas_call(
        iteration_kernel,
        out_shape=jax.ShapeDtypeStruct((blocks * tile, width), jnp.float32),
        in_specs=[pl.BlockSpec(memory_space=pltpu.SMEM)] * 3
        + [pl.BlockSpec(memory_space=pltpu.VMEM)]
        + [pl.BlockSpec(memory_space=pltpu.HBM)] * 2,
        out_specs=pl.BlockSpec(memory_space=pltpu.VMEM),
        scratch_shapes=[
            pltpu.VMEM(tiles_near.shape, tiles_near.dtype),
            pltpu.VMEM(tiles_far.shape, tiles_far.dtype),
            pltpu.VMEM((NG, tile, width), start.dtype),
            pltpu.VMEM((NC, SIDE, SIDE, 8, 128), jnp.float32),
            pltpu.VMEM((NC * SIDE, SIDE, 8, 128), jnp.float32),
            pltpu.VMEM((blocks * tile, width), jnp.float32),
            pltpu.VMEM((LINE, rows, width), jnp.float32),
            pltpu.VMEM((width, 2 * width), jnp.float32),
            pltpu.VMEM((width, width), jnp.float32),
        ]
        + step_buffers * ITERS
        + [
            pltpu.SemaphoreType.DMA((2,)),
            pltpu.SemaphoreType.DMA((2,)),
            pltpu.SemaphoreType.DMA((ITERS, 2, NZ // 2, 2)),
            pltpu.SemaphoreType.DMA,
            pltpu.SemaphoreType.DMA,
            pltpu.SemaphoreType.DMA,
            pltpu.SemaphoreType.DMA((ITERS, SIDE - 1)),
            pltpu.SemaphoreType.DMA,
            pltpu.SemaphoreType.DMA((ITERS,)),
            pltpu.SemaphoreType.DMA((3,)),
            pltpu.SemaphoreType.DMA((ITERS, 3)),
        ],
        compiler_params=pltpu.CompilerParams(
            collective_id=0, has_side_effects=True, vmem_limit_bytes=60 << 20
        ),
        name="iterate",
    )(near_cols, far_groups, need, start, tiles_near, tiles_far)


def per_device(tiles_near, near_cols, tiles_far, far_groups, need_blocks, start_vectors):
    tile_size = tiles_near.shape[1]
    rows, vec_width = start_vectors.shape
    start = start_vectors.reshape(rows // tile_size, tile_size, vec_width)
    return iterate(near_cols, far_groups, need_blocks, start, tiles_near, tiles_far)


def solution(mesh):
    in_specs = (
        P(("grp", "blk"), None, None),
        P(("grp", "blk"), None),
        P(("grp", "blk"), None, None),
        P(("grp", "blk"), None),
        P(("grp", "blk"), None),
        P(("grp", "blk"), None),
    )
    out_specs = P(("grp", "blk"), None)
    return jax.shard_map(
        per_device, mesh=mesh, in_specs=in_specs, out_specs=out_specs, check_vma=False
    )
```

```python
import jax
import jax.numpy as jnp
from jax import lax
from jax.experimental import pallas as pl
from jax.experimental.pallas import tpu as pltpu
from jax.sharding import PartitionSpec as P

ITERS = 2
MESH = pl.DeviceIdType.MESH
NX, NY, NC, NZ = 4, 4, 2, 8
NG = NX * NY * NC
LINE = NC * NZ
PLANE = NX * NY
PANEL = 16
SIDE = NX
STEP_BUFFERS = NZ + SIDE - 1 + 6
FAR_IN = SIDE * (NC * SIDE - 1)


def wait_bytes(ref, sem):
    pltpu.make_async_copy(ref, ref, sem).wait()


def split(value):
    high = value.astype(jnp.bfloat16)
    rest = value - high.astype(jnp.float32)
    middle = rest.astype(jnp.bfloat16)
    return high, middle, (rest - middle.astype(jnp.float32)).astype(jnp.bfloat16)


def inverse_factor(gram, work, out):
    n = gram.shape[0]
    row_id = lax.broadcasted_iota(jnp.int32, (n, n), 0)
    col_id = lax.broadcasted_iota(jnp.int32, (n, n), 1)
    work[:, :n] = gram
    work[:, n:] = (row_id == col_id).astype(jnp.float32)
    sub = lax.broadcasted_iota(jnp.int32, (8, 2 * n), 0)

    def wide(value):
        return jnp.concatenate([value] * 2, 1)

    def panel(p, carry):
        start = pl.multiple_of(p * PANEL, PANEL)
        rows = pl.ds(start, PANEL)
        top = work[rows, :]
        diag = pltpu.roll(top[:, :n], lax.rem(n - start, n), 1)
        a, low, scale, solved = {}, {}, [], []
        for j in range(PANEL):
            for i in range(j, PANEL):
                a[i, j] = jnp.broadcast_to(diag[i : i + 1, j : j + 1], (8, n))
        for j in range(PANEL):
            scale.append(lax.rsqrt(a[j, j]))
            for i in range(j + 1, PANEL):
                low[i, j] = a[i, j] * scale[j]
            for k in range(j + 1, PANEL):
                for i in range(k, PANEL):
                    a[i, k] = a[i, k] - low[i, j] * low[k, j]
        for j in range(PANEL):
            row = jnp.broadcast_to(top[j : j + 1, :], (8, 2 * n))
            for k in range(j):
                row = row - wide(low[j, k]) * solved[k]
            solved.append(row * wide(scale[j]))
        pieces = []
        for b in range(0, PANEL, 8):
            piece = solved[b]
            for j in range(1, 8):
                piece = jnp.where(sub == j, solved[b + j], piece)
            pieces.append(piece)
        block = jnp.concatenate(pieces, 0)
        out[rows, :] = block[:, n:]
        high, middle, small = split(block)
        left = jnp.concatenate([v[:, :n] for v in (high, high, middle, high, small, middle)], 0)
        right = jnp.concatenate([high, middle, high, small, high, middle], 0)
        work[...] = work[...] - lax.dot_general(
            left, right, (((0,), (0,)), ((), ())), preferred_element_type=jnp.float32
        )
        return carry

    lax.fori_loop(0, n // PANEL, panel, 0)


def iteration_kernel(*refs):
    (near_cols, far_groups, need, start, tiles_near, tiles_far, vectors_out,
     a_near, a_far, stage, request, wanted, product, gram, work, inverse) = refs[:16]
    refs = refs[16:]
    per_step = [refs[i * STEP_BUFFERS : (i + 1) * STEP_BUFFERS] for i in range(ITERS)]
    (tile_sem, ring_send, ring_recv, req_send, req_recv, share_send, share_recv, far_send, far_recv,
     ar_send, ar_recv) = refs[ITERS * STEP_BUFFERS :]

    g = lax.axis_index("grp")
    z = lax.axis_index("blk")
    core = lax.rem(g, NC)
    xy = g // NC
    x, y = xy // NY, lax.rem(xy, NY)
    blocks, tile, width = start.shape
    half = blocks // 2
    rows_each = width // LINE
    q = z * NC + core

    load_near = pltpu.make_async_copy(tiles_near, a_near, tile_sem.at[0])
    load_far = pltpu.make_async_copy(tiles_far, a_far, tile_sem.at[1])
    load_near.start()
    load_far.start()

    def group_at(first, second, which):
        px = first + which * (second - first)
        py = second + which * (first - second)
        return px * NY + py

    axis_a = x + core * (y - x)
    axis_b = y + core * (x - y)

    def same_core(first, second):
        return group_at(first, second, core) * NC + core

    def line_peer(k):
        pz, pc = lax.rem(z + k // NC, NZ), lax.rem(core + (k % NC), NC)
        return xy * NC + pc, pz

    def plane_peer(k):
        px, py = lax.rem(x + k // NY, NX), lax.rem(y + (k % NY), NY)
        return (px * NY + py) * NC + core

    line_order = sorted(range(1, LINE), key=lambda k: -min(k // NC, NZ - k // NC))
    plane_order = sorted(
        range(1, PLANE), key=lambda k: -min(k // NY, NX - k // NY) - min(k % NY, NY - k % NY)
    )
    barrier = pltpu.get_barrier_semaphore()

    def greet(group, position):
        pl.semaphore_signal(barrier, inc=1, device_id=(group, position), device_id_type=MESH)

    def greet_line(k, carry):
        greet(*line_peer(k))
        return carry

    def greet_plane(k, carry):
        greet(plane_peer(k), z)
        return carry

    def greet_cross(k, carry):
        greet(group_at(axis_a, lax.rem(axis_b + k, SIDE), core) * NC + 1 - core, z)
        greet(group_at(lax.rem(axis_a + k, SIDE), axis_b, core) * NC + 1 - core, z)
        return carry

    lax.fori_loop(1, LINE, greet_line, 0)
    lax.fori_loop(1, PLANE, greet_plane, 0)
    lax.fori_loop(1, SIDE, greet_cross, 0)

    def fill_request(k, carry):
        t, b, a = k // (SIDE * SIDE), lax.rem(k // SIDE, SIDE), lax.rem(k, SIDE)
        source = group_at(a, b, t) * NC + t
        value = jnp.full(request.shape[3:], need[0, source], jnp.int32).astype(jnp.float32)
        request[t, b, a] = value
        return carry

    lax.fori_loop(0, NG, fill_request, 0)
    wanted[axis_b * NC + core] = request[core, axis_b]
    per_step[0][0][...] = start[...]
    pl.semaphore_wait(barrier, LINE - 1 + PLANE - 1 + 2 * (SIDE - 1))

    right, left = lax.rem(z + 1, NZ), lax.rem(z + NZ - 1, NZ)
    last = NZ // 2 - 1

    def parts(direction, step):
        if step < last:
            return (0, 1) if direction == 0 else (1, 0)
        return (direction,)

    def send_request(k, carry):
        t = lax.rem(core + k // SIDE, NC)
        mine_a, mine_b = x + t * (y - x), y + t * (x - y)
        b = lax.rem(mine_b + lax.rem(k, SIDE), SIDE)
        relay = group_at(mine_a, b, t) * NC + t
        pltpu.make_async_remote_copy(
            src_ref=request.at[t, b], dst_ref=wanted.at[mine_b * NC + core],
            send_sem=req_send, recv_sem=req_recv,
            device_id=(relay, z), device_id_type=MESH,
        ).start()
        return carry

    near_row = a_near.shape[0] // blocks
    per_source = near_row // NZ
    far_row = a_far.shape[0] // blocks

    for it in range(ITERS):
        own, away = per_step[it][0], per_step[it][1 : NZ]
        relay_buf = per_step[it][NZ : NZ + SIDE - 1]
        far_buf, rs_buf, part, plane_buf, total, gathered = per_step[it][NZ + SIDE - 1 :]

        def slot(direction, step):
            return away[2 * last] if step == last else away[2 * step + direction]

        def ring(direction, step, part_id):
            rows = pl.ds(part_id * half, half)
            src = own if step == 0 else slot(direction, step - 1)
            return pltpu.make_async_remote_copy(
                src_ref=src.at[rows],
                dst_ref=slot(direction, step).at[rows],
                send_sem=ring_send.at[direction],
                recv_sem=ring_recv.at[it, direction, step, part_id],
                device_id=(g, left if direction else right),
                device_id_type=MESH,
            )

        for i in range(2):
            for direction in (0, 1):
                ring(direction, 0, parts(direction, 0)[i]).start()

        if it == 0:
            lax.fori_loop(1, 2 * SIDE, send_request, 0)

        def share(k):
            return pltpu.make_async_remote_copy(
                src_ref=own, dst_ref=relay_buf[SIDE - k - 1],
                send_sem=share_send, recv_sem=share_recv.at[it, SIDE - k - 1],
                device_id=(same_core(lax.rem(axis_a + k, SIDE), axis_b), z), device_id_type=MESH,
            )

        for k in (1, 3, 2):
            share(k).start()
        if it == 0:
            wait_bytes(wanted.at[pl.ds(0, NC * SIDE - 1)], req_recv)

        def choose(shard, ask):
            choice = ask[None]
            picked = shard[0].astype(jnp.float32).reshape(-1, 8, 128)
            for b in range(1, blocks):
                other = shard[b].astype(jnp.float32).reshape(-1, 8, 128)
                picked = jnp.where(choice == float(b), other, picked)
            return picked.reshape(tile, width).astype(start.dtype)

        def pass_on(away_by):
            shard = own if away_by == 0 else relay_buf[away_by - 1]
            a = lax.rem(axis_a + away_by, SIDE)
            source = same_core(a, axis_b)

            def send_one(m, carry):
                b, c = lax.rem(axis_b + m // NC, SIDE), lax.rem(core + lax.rem(m, NC), NC)
                spot = away_by * (NC * SIDE - 1) + m - 1
                stage[spot] = choose(shard, wanted[b * NC + c, a])
                pltpu.make_async_remote_copy(
                    src_ref=stage.at[spot], dst_ref=far_buf.at[source],
                    send_sem=far_send, recv_sem=far_recv.at[it],
                    device_id=(group_at(axis_a, b, core) * NC + c, z), device_id_type=MESH,
                ).start()
                return carry

            lax.fori_loop(1, NC * SIDE, send_one, 0)
            far_buf[source] = choose(shard, wanted[axis_b * NC + core, a])

        pass_on(0)

        def near_part(shard, source, first):
            def one_row(r, carry):
                rows = pl.ds(pl.multiple_of(r * tile, tile), tile)
                acc = None if first else product[rows, :]
                for n in range(per_source):
                    t = r * near_row + source * per_source + n
                    term = jnp.dot(
                        a_near[t], shard[near_cols[0, t]], preferred_element_type=jnp.float32
                    )
                    acc = term if acc is None else acc + term
                product[rows, :] = acc
                return carry

            lax.fori_loop(0, blocks, one_row, 0, unroll=True)

        def far_rows(r, carry):
            rows = pl.ds(pl.multiple_of(r * tile, tile), tile)
            acc = product[rows, :]
            for j in range(far_row):
                t = r * far_row + j
                acc += jnp.dot(
                    a_far[t], far_buf[far_groups[0, t]], preferred_element_type=jnp.float32
                )
            product[rows, :] = acc
            return carry

        def forward(step):
            for i in range(2):
                for direction in (0, 1):
                    if i < len(parts(direction, step)):
                        here = parts(direction, step)[i]
                        ring(direction, step, here).wait_recv()
                        if step < last and here in parts(direction, step + 1):
                            ring(direction, step + 1, here).start()

        if it == 0:
            load_near.wait()
            load_far.wait()
        near_part(own, z, True)
        forward(0)
        for k in (1, 3, 2):
            share(SIDE - k).wait_recv()
            pass_on(k)
        for step in range(last):
            if step:
                forward(step)
            near_part(slot(0, step), lax.rem(z + NZ - 1 - step, NZ), False)
            near_part(slot(1, step), lax.rem(z + 1 + step, NZ), False)
        wait_bytes(far_buf.at[pl.ds(0, FAR_IN)], far_recv.at[it])
        lax.fori_loop(0, blocks, far_rows, 0, unroll=True)
        forward(last)
        near_part(slot(0, last), lax.rem(z + NZ // 2, NZ), False)

        flat = product[...]
        gram[...] = lax.dot_general(
            flat, flat, (((0,), (0,)), ((), ())),
            precision=lax.Precision.HIGHEST, preferred_element_type=jnp.float32,
        ).reshape(gram.shape)

        def scatter(k, carry):
            pg, pz = line_peer(k)
            pltpu.make_async_remote_copy(
                src_ref=gram.at[pz * NC + lax.rem(pg, NC)], dst_ref=rs_buf.at[q],
                send_sem=ar_send.at[0], recv_sem=ar_recv.at[it, 0],
                device_id=(pg, pz), device_id_type=MESH,
            ).start()
            return carry

        for k in line_order:
            scatter(k, 0)
        rs_buf[q] = gram[q]
        wait_bytes(rs_buf.at[pl.ds(0, LINE - 1)], ar_recv.at[it, 0])
        part[...] = jnp.sum(rs_buf[...], axis=0)
        plane_buf[xy] = part[...]

        def spread(k, carry):
            pltpu.make_async_remote_copy(
                src_ref=part, dst_ref=plane_buf.at[xy],
                send_sem=ar_send.at[1], recv_sem=ar_recv.at[it, 1],
                device_id=(plane_peer(k), z), device_id_type=MESH,
            ).start()
            return carry

        for k in plane_order:
            spread(k, 0)
        wait_bytes(plane_buf.at[pl.ds(0, PLANE - 1)], ar_recv.at[it, 1])
        total[...] = jnp.sum(plane_buf[...], axis=0)
        gathered[q] = total[...]

        def collect(k, carry):
            pltpu.make_async_remote_copy(
                src_ref=total, dst_ref=gathered.at[q],
                send_sem=ar_send.at[2], recv_sem=ar_recv.at[it, 2],
                device_id=line_peer(k), device_id_type=MESH,
            ).start()
            return carry

        for k in line_order:
            collect(k, 0)
        wait_bytes(gathered.at[pl.ds(0, LINE - 1)], ar_recv.at[it, 2])

        sent = (last + 1) * blocks - half
        for direction in (0, 1):
            wait_bytes(far_buf.at[pl.ds(0, sent)], ring_send.at[direction])
        if it == 0:
            wait_bytes(wanted.at[pl.ds(0, NC * SIDE - 1)], req_send)
        wait_bytes(stage.at[pl.ds(0, FAR_IN)], far_send)
        wait_bytes(stage.at[pl.ds(0, (SIDE - 1) * blocks)], share_send)
        wait_bytes(rs_buf.at[pl.ds(0, LINE - 1)], ar_send.at[0])
        wait_bytes(plane_buf.at[pl.ds(0, PLANE - 1)], ar_send.at[1])
        wait_bytes(gathered.at[pl.ds(0, LINE - 1)], ar_send.at[2])

        total_rows = float(blocks * tile * NG * NZ)
        inverse_factor(gathered[...].reshape(width, width) / total_rows, work, inverse)

        def make_vectors(r, carry):
            rows = pl.ds(pl.multiple_of(r * tile, tile), tile)
            block = lax.dot_general(
                product[rows, :], inverse[...], (((1,), (1,)), ((), ())),
                precision=lax.Precision.HIGHEST, preferred_element_type=jnp.float32,
            )
            if it == ITERS - 1:
                vectors_out[rows, :] = block
            else:
                per_step[it + 1][0][r] = block.astype(start.dtype)
            return carry

        lax.fori_loop(0, blocks, make_vectors, 0, unroll=True)


def iterate(near_cols, far_groups, need, start, tiles_near, tiles_far):
    blocks, tile, width = start.shape
    rows = width // LINE
    step_buffers = (
        [pltpu.VMEM((blocks, tile, width), start.dtype)] * (NZ + SIDE - 1)
        + [
            pltpu.VMEM((NG, tile, width), start.dtype),
            pltpu.VMEM((LINE, rows, width), jnp.float32),
            pltpu.VMEM((rows, width), jnp.float32),
            pltpu.VMEM((PLANE, rows, width), jnp.float32),
            pltpu.VMEM((rows, width), jnp.float32),
            pltpu.VMEM((LINE, rows, width), jnp.float32),
        ]
    )
    assert len(step_buffers) == STEP_BUFFERS
    return pl.pallas_call(
        iteration_kernel,
        out_shape=jax.ShapeDtypeStruct((blocks * tile, width), jnp.float32),
        in_specs=[pl.BlockSpec(memory_space=pltpu.SMEM)] * 3
        + [pl.BlockSpec(memory_space=pltpu.VMEM)]
        + [pl.BlockSpec(memory_space=pltpu.HBM)] * 2,
        out_specs=pl.BlockSpec(memory_space=pltpu.VMEM),
        scratch_shapes=[
            pltpu.VMEM(tiles_near.shape, tiles_near.dtype),
            pltpu.VMEM(tiles_far.shape, tiles_far.dtype),
            pltpu.VMEM((NG, tile, width), start.dtype),
            pltpu.VMEM((NC, SIDE, SIDE, 8, 128), jnp.float32),
            pltpu.VMEM((NC * SIDE, SIDE, 8, 128), jnp.float32),
            pltpu.VMEM((blocks * tile, width), jnp.float32),
            pltpu.VMEM((LINE, rows, width), jnp.float32),
            pltpu.VMEM((width, 2 * width), jnp.float32),
            pltpu.VMEM((width, width), jnp.float32),
        ]
        + step_buffers * ITERS
        + [
            pltpu.SemaphoreType.DMA((2,)),
            pltpu.SemaphoreType.DMA((2,)),
            pltpu.SemaphoreType.DMA((ITERS, 2, NZ // 2, 2)),
            pltpu.SemaphoreType.DMA,
            pltpu.SemaphoreType.DMA,
            pltpu.SemaphoreType.DMA,
            pltpu.SemaphoreType.DMA((ITERS, SIDE - 1)),
            pltpu.SemaphoreType.DMA,
            pltpu.SemaphoreType.DMA((ITERS,)),
            pltpu.SemaphoreType.DMA((3,)),
            pltpu.SemaphoreType.DMA((ITERS, 3)),
        ],
        compiler_params=pltpu.CompilerParams(
            collective_id=0, has_side_effects=True, vmem_limit_bytes=60 << 20
        ),
        name="iterate",
    )(near_cols, far_groups, need, start, tiles_near, tiles_far)


def per_device(tiles_near, near_cols, tiles_far, far_groups, need_blocks, start_vectors):
    tile_size = tiles_near.shape[1]
    rows, vec_width = start_vectors.shape
    start = start_vectors.reshape(rows // tile_size, tile_size, vec_width)
    return iterate(near_cols, far_groups, need_blocks, start, tiles_near, tiles_far)


def solution(mesh):
    in_specs = (
        P(("grp", "blk"), None, None),
        P(("grp", "blk"), None),
        P(("grp", "blk"), None, None),
        P(("grp", "blk"), None),
        P(("grp", "blk"), None),
        P(("grp", "blk"), None),
    )
    out_specs = P(("grp", "blk"), None)
    return jax.shard_map(
        per_device, mesh=mesh, in_specs=in_specs, out_specs=out_specs, check_vma=False
    )
```
